512 devices in a mesh: segment: 4 (over z_lo), row: 16 (over y, z_hi), col: 8 (over x, core).
Axes of the slice: x: 4, y: 8, z: 8 (z_hi: 2, z_lo: 4; z = z_hi * 4 + z_lo), core: 2. Of those that a mesh axis runs over, the one named last changes fastest.
Arguments:
- frames: bfloat16 [2, 256, 128, 128], P(None, 'row', 'col'), may hold values from -6 to 6
- caches: bfloat16 [4, 2, 2, 256, 128, 128], P('segment', None, None, 'row', 'col'), may hold values from -5 to 5
- weights: bfloat16 [4, 2, 3, 3, 3, 128, 128], P('segment'), may hold values from -0.109375 to 0.109375
- biases: float32 [4, 2, 128], P('segment'), may hold values from -0.5 to 0.5
- gains: float32 [4, 2, 128], P('segment'), may hold values from 0.1 to 1.9
Outputs:
- sections: bfloat16 [4, 2, 256, 128, 128], P('segment', None, 'row', 'col')
The draws below stay inside these ranges and needn't reach their ends.
All inputs are finite; a program needn't handle non-finite values.
Results may differ from the reference program's by a relative error of at most 0.0055.
Values may be sent and summed in bfloat16 or wider, within the bound.
No kernel may reach another device: no remote copies, remote signals or barrier semaphores. Data moves between devices by JAX's collectives and lax.ppermute only.
A program may use at most 64 MiB of HBM per device.

```python
import jax
import jax.numpy as jnp
from jax import lax

C = 128
SECTIONS = 4
FRAMES = 2
H = 256
W = 128
N_SEGMENT = 4


def shard_levels(key, shape, pieces, smallest, high):
    loudness, own = 1.0, jax.random.fold_in(key, 6)
    for position, shards_of in pieces:
        draws = jnp.exp(jax.random.uniform(jax.random.fold_in(own, position), (shards_of,), jnp.float32, smallest / len(pieces), high / len(pieces)))
        loudness = loudness * jnp.repeat(draws, shape[position] // shards_of).reshape([-1 if axis == position else 1 for axis in range(len(shape))])
    return loudness


def centred(own_key, extent, spread, limit, shards=(), dtype=jnp.bfloat16):
    entries = jax.random.normal(own_key, extent, jnp.float32) * spread
    if len(shards) > 0:
        entries = shard_levels(own_key, extent, shards, -0.22, 0.18) * entries
    return jnp.clip(entries, min=-limit, max=limit).astype(dtype)


def setup_inputs(seed: int = 0) -> dict:
    streams_of = jax.random.split(jax.random.key(seed), 6)
    return {
        "frames": centred(streams_of[0], (FRAMES, H, W, C), 1.0, 6.0, ((1, 16), (2, 8))),
        "caches": centred(streams_of[1], (SECTIONS, 2, 2, H, W, C), 0.7, 5.0, ((0, 4), (3, 16), (4, 8))),
        "weights": centred(streams_of[2], (SECTIONS, 2, 3, 3, 3, C, C), (27 * C) ** -0.5, 0.109375, ((0, 4),)),
        "biases": jnp.clip(jax.random.uniform(streams_of[3], (SECTIONS, 2, C), jnp.float32, -0.5, 0.5) * shard_levels(streams_of[3], (SECTIONS, 2, C), ((0, 4),), -0.4, 0.0), -0.5, 0.5),
        "gains": jnp.clip(1.0 + 0.18 * jax.random.normal(streams_of[4], (SECTIONS, 2, C), jnp.float32), 0.1, 1.9),
    }


def norm_act(values, gain_row):
    values = values.astype(jnp.float32)
    scaled = values * jax.lax.rsqrt(lax.optimization_barrier(jnp.mean(values * values, axis=-1, keepdims=True)) + 1e-06) * gain_row
    return jax.nn.silu(scaled).astype(jnp.bfloat16)

def convolve(sequence, previous, kernel, bias_row):
    joined = jnp.concatenate([previous, sequence], axis=0)
    padded = jnp.pad(joined, ((0, 0), (1, 1), (1, 1), (0, 0)))
    frame_count = sequence.shape[0]
    rows = sequence.shape[1]
    cols = sequence.shape[2]
    accum = jnp.zeros(sequence.shape[:3] + (kernel.shape[-1],), jnp.float32)
    for tap_t in range(3):
        for tap_h in range(3):
            for tap_w in range(3):
                slab = padded[tap_t:tap_t + frame_count, tap_h:tap_h + rows, tap_w:tap_w + cols].astype(jnp.float32)
                accum = accum + jnp.einsum('fhwc,co->fhwo', slab, kernel[tap_t, tap_h, tap_w].astype(jnp.float32))
    return accum + bias_row

def reference(frames, caches, weights, biases, gains):
    current = frames
    results = []
    for section in range(N_SEGMENT):
        normed_one = norm_act(current, gains[section, 0])
        hidden = convolve(normed_one, caches[section, 0], weights[section, 0], biases[section, 0])
        normed_two = norm_act(hidden, gains[section, 1])
        branch = convolve(normed_two, caches[section, 1], weights[section, 1], biases[section, 1])
        current = (current.astype(jnp.float32) + branch).astype(jnp.bfloat16)
        results.append(current)
    return jnp.stack(results, axis=0)
```

```python
import functools

import jax
import jax.numpy as jnp
from jax import lax
from jax.experimental import pallas as pl
from jax.experimental.pallas import tpu as pltpu
from jax.sharding import PartitionSpec as P

PITCH = 32
CHUNK = 8
AXES = ("segment", "row", "col")


def norm_act(values, gain_row, mask):
    scale = lax.rsqrt(jnp.mean(values * values, axis=-1, keepdims=True) + 1e-06)
    scaled = values * scale * gain_row
    return scaled / (1.0 + jnp.exp(-scaled)) * mask


def chunks(rows):
    return [(first, min(CHUNK, rows - first)) for first in range(0, rows, CHUNK)]


def column_mask(side, width, channels):
    col = lax.broadcasted_iota(jnp.int32, (PITCH, channels), 0) + side
    return jnp.where((col >= 0) & (col < width), 1.0, 0.0)


def cell_mask(columns, top, height, first, count):
    parts = []
    for row in range(first, first + count):
        here = top + row
        parts.append(columns * jnp.where((here >= 0) & (here < height), 1.0, 0.0))
    return jnp.concatenate(parts, axis=0)


def spread(source, start, patches, block, rows):
    channels = source.shape[-1]
    for tap in range(3):
        lane = (block * 3 + tap) * channels
        begin = start + tap
        patches[: rows * PITCH, lane : lane + channels] = source[
            begin : begin + rows * PITCH, :
        ].astype(jnp.bfloat16)


def weight_rows(kernel, tap, left, right):
    empty = jnp.zeros(kernel.shape[2:], jnp.bfloat16)

    def column(taps):
        return jnp.concatenate(
            [empty if t is None else kernel[t, tap] for t in taps], axis=0
        )

    return jnp.concatenate([column(left), column(right)], axis=1)


BOTH = ((0, 1, 2, None), (None, 0, 1, 2))
HELD = ((0, 1), (None, 0))
FRESH = ((2, None), (1, 2))


def convolve(patches, kernel, taps, total, first, rows):
    count = rows * PITCH
    for tap in range(3):
        begin = (first + tap) * PITCH
        total = total + jnp.dot(
            patches[begin : begin + count, :],
            weight_rows(kernel, tap, *taps),
            preferred_element_type=jnp.float32,
        )
    return total


def bias_of(bias, count):
    return jnp.broadcast_to(
        jnp.concatenate([bias, bias], axis=1), (count, 2 * bias.shape[-1])
    )


def assemble(grid, frame, source, mid, low, high, left, right):
    reach = low.shape[1]
    tile = mid.shape[1]
    for row in range(tile + 2 * reach):
        begin = row * PITCH
        if row < reach:
            body = low[source, row]
        elif row < reach + tile:
            body = mid[source, row - reach]
        else:
            body = high[source, row - reach - tile]
        grid[frame, begin : begin + reach, :] = left[source, row].astype(jnp.float32)
        grid[frame, begin + reach : begin + reach + tile, :] = body.astype(jnp.float32)
        grid[frame, begin + reach + tile : begin + 2 * reach + tile, :] = right[
            source, row
        ].astype(jnp.float32)


def finish(step, place, halo, span, first, count, branch, held, o_ref, r_ref):
    channels = held.shape[-1]
    tile = r_ref.shape[2]
    edge = halo - 2
    for frame in range(2):
        offset = (first + 2) * PITCH + 2
        out = (
            held[frame, offset : offset + count * PITCH, :]
            + branch[:, frame * channels : (frame + 1) * channels]
        )
        for row in range(count):
            line = out[row * PITCH : (row + 1) * PITCH]
            if o_ref is not None:
                o_ref[frame, first + row] = line[: span - 4].astype(jnp.bfloat16)
            own = first + row - edge
            if 0 <= own < tile:
                cells = line[edge : edge + tile].astype(jnp.bfloat16)
                if step == 0:
                    r_ref[frame, own] = cells
                else:

                    @pl.when(place[2] == step)
                    def _(frame=frame, own=own, cells=cells):
                        r_ref[frame, own] = cells


def middle(place, halo, height, width, hidden_of, g_ref, flat, span):
    channels = g_ref.shape[-1]
    tile = span - 2 * halo
    top = place[0] * tile - (halo - 1)
    columns = column_mask(place[1] * tile - (halo - 1), width, channels)
    for first, count in chunks(span - 2):
        hidden = hidden_of(first, count)
        keep = cell_mask(columns, top, height, first, count)
        for frame in range(2):
            flat[frame, first * PITCH : (first + count) * PITCH, :] = norm_act(
                hidden[:, frame * channels : (frame + 1) * channels], g_ref[1:2, :], keep
            )


def entry(place, halo, height, width, held, g_ref, flat, span):
    channels = g_ref.shape[-1]
    tile = span - 2 * halo
    top = place[0] * tile - halo
    columns = column_mask(place[1] * tile - halo, width, channels)
    for first, count in chunks(span):
        area = pl.ds(first * PITCH, count * PITCH)
        keep = cell_mask(columns, top, height, first, count)
        for frame in range(2):
            flat[frame, area, :] = norm_act(held[frame, area, :], g_ref[0:1, :], keep)


def first_kernel(
    halo, height, width, place, frames, cached, low, high, left, right, w_ref, b_ref, g_ref,
    o_ref, r_ref, grid, flat, patches,
):
    tile = frames.shape[1]
    span = tile + 2 * halo
    for frame in range(2):
        assemble(grid, frame, frame, frames, low, high, left, right)
    for frame in range(4):
        assemble(
            grid, frame + 2, frame, cached, low.at[2:6], high.at[2:6],
            left.at[2:6], right.at[2:6],
        )
    entry(place, halo, height, width, grid, g_ref, flat, span)
    for frame in range(2):
        spread(grid.at[frame + 2], 0, patches, frame, span)
        spread(flat.at[frame], 0, patches, frame + 2, span)
    middle(
        place, halo, height, width,
        lambda first, count: convolve(
            patches, w_ref.at[0], BOTH, bias_of(b_ref[0:1, :], count * PITCH), first, count
        ),
        g_ref, flat, span,
    )
    for frame in range(2):
        spread(grid.at[frame + 4], PITCH + 1, patches, frame, span - 2)
        spread(flat.at[frame], 0, patches, frame + 2, span - 2)
    for first, count in chunks(span - 4):
        branch = convolve(
            patches, w_ref.at[1], BOTH, bias_of(b_ref[1:2, :], count * PITCH), first, count
        )
        finish(0, place, halo, span, first, count, branch, grid, o_ref, r_ref)


def held_kernel(
    cached, low, high, left, right, w_ref, b_ref, one_ref, two_ref, grid, patches
):
    span = cached.shape[1] + 2 * low.shape[1]
    for frame in range(4):
        assemble(grid, frame, frame, cached, low, high, left, right)
    for conv, out in ((0, one_ref), (1, two_ref)):
        start = conv * (PITCH + 1)
        rows = span - 2 * conv
        for frame in range(2):
            spread(grid.at[2 * conv + frame], start, patches, frame, rows)
        for first, count in chunks(rows - 2):
            out[first * PITCH : (first + count) * PITCH, :] = convolve(
                patches, w_ref.at[conv], HELD,
                bias_of(b_ref[conv : conv + 1, :], count * PITCH), first, count,
            )


def later_kernel(
    step, halo, drop, height, width, place, x_ref, one_ref, two_ref, w_ref, g_ref, p_ref,
    *rest,
):
    o_ref = rest[0] if len(rest) == 5 else None
    r_ref, held, flat, patches = rest[-4:]
    span = x_ref.shape[1]
    r_ref[...] = p_ref[...]
    for frame in range(2):
        for row in range(span):
            held[frame, row * PITCH : row * PITCH + span, :] = x_ref[frame, row].astype(
                jnp.float32
            )
    entry(place, halo, height, width, held, g_ref, flat, span)
    for frame in range(2):
        spread(flat.at[frame], 0, patches, frame, span)

    def known(ref, first, count):
        begin = drop * (PITCH + 1) + first * PITCH
        return ref[begin : begin + count * PITCH, :]

    middle(
        place, halo, height, width,
        lambda first, count: convolve(
            patches, w_ref.at[0], FRESH, known(one_ref, first, count), first, count
        ),
        g_ref, flat, span,
    )
    for frame in range(2):
        spread(flat.at[frame], 0, patches, frame, span - 2)
    for first, count in chunks(span - 4):
        branch = convolve(
            patches, w_ref.at[1], FRESH, known(two_ref, first, count), first, count
        )
        finish(step, place, halo, span, first, count, branch, held, o_ref, r_ref)


SCALARS = pl.BlockSpec(memory_space=pltpu.SMEM)
WHOLE = pl.BlockSpec(memory_space=pltpu.VMEM)


def cost(span, frames, channels):
    return pl.CostEstimate(
        flops=4 * 9 * frames * span * PITCH * channels * 2 * channels,
        bytes_accessed=4 << 20,
        transcendentals=0,
    )


def first_section(place, frames, cached, pieces, weights, biases, gains, halo, height, width):
    tile, channels = frames.shape[1], frames.shape[-1]
    span = tile + 2 * halo
    room = span * PITCH + 3 * PITCH
    return pl.pallas_call(
        functools.partial(first_kernel, halo, height, width),
        out_shape=(
            jax.ShapeDtypeStruct((2, span - 4, span - 4, channels), jnp.bfloat16),
            jax.ShapeDtypeStruct(frames.shape, jnp.bfloat16),
        ),
        in_specs=[SCALARS] + [WHOLE] * 9,
        out_specs=(WHOLE, WHOLE),
        scratch_shapes=[
            pltpu.VMEM((6, room, channels), jnp.float32),
            pltpu.VMEM((2, room, channels), jnp.float32),
            pltpu.VMEM((room, 12 * channels), jnp.bfloat16),
        ],
        cost_estimate=cost(span, 4, channels),
        compiler_params=pltpu.CompilerParams(vmem_limit_bytes=40 << 20),
    )(place, frames, cached, *pieces, weights, biases, gains)


def held_part(cached, pieces, weights, biases):
    channels = cached.shape[-1]
    span = cached.shape[1] + 2 * pieces[0].shape[1]
    room = span * PITCH + 3 * PITCH
    return pl.pallas_call(
        held_kernel,
        out_shape=(
            jax.ShapeDtypeStruct(((span - 2) * PITCH, 2 * channels), jnp.float32),
            jax.ShapeDtypeStruct(((span - 4) * PITCH, 2 * channels), jnp.float32),
        ),
        in_specs=[WHOLE] * 7,
        out_specs=(WHOLE, WHOLE),
        scratch_shapes=[
            pltpu.VMEM((4, room, channels), jnp.float32),
            pltpu.VMEM((room, 6 * channels), jnp.bfloat16),
        ],
        cost_estimate=cost(span, 2, channels),
        compiler_params=pltpu.CompilerParams(vmem_limit_bytes=40 << 20),
    )(cached, *pieces, weights, biases)


def later_section(
    step, place, values, known, weights, gains, results, halo, drop, last, height, width
):
    span, channels = values.shape[1], values.shape[-1]
    room = span * PITCH + 3 * PITCH
    out_shape = [jax.ShapeDtypeStruct(results.shape, jnp.bfloat16)]
    if not last:
        onward = (2, span - 4, span - 4, channels)
        out_shape = [jax.ShapeDtypeStruct(onward, jnp.bfloat16)] + out_shape
    return pl.pallas_call(
        functools.partial(later_kernel, step, halo, drop, height, width),
        out_shape=out_shape,
        in_specs=[SCALARS] + [WHOLE] * 6,
        out_specs=[WHOLE] * len(out_shape),
        scratch_shapes=[
            pltpu.VMEM((2, room, channels), jnp.float32),
            pltpu.VMEM((2, room, channels), jnp.float32),
            pltpu.VMEM((room, 6 * channels), jnp.bfloat16),
        ],
        cost_estimate=cost(span, 2, channels),
        compiler_params=pltpu.CompilerParams(vmem_limit_bytes=40 << 20),
    )(place, values, *known, weights, gains, results)


def moved(value, segments, shift):
    sizes = [lax.axis_size(axis) for axis in AXES]
    pairs = []
    for segment in segments:
        for row in range(sizes[1]):
            for col in range(sizes[2]):
                target = (segment + shift[0], row + shift[1], col + shift[2])
                if all(0 <= t < n for t, n in zip(target, sizes)):
                    source = (segment * sizes[1] + row) * sizes[2] + col
                    place = (target[0] * sizes[1] + target[1]) * sizes[2] + target[2]
                    pairs.append((source, place))
    return lax.ppermute(value, AXES, pairs)


def ends(parts, cut):
    taken = [cut(part) for part in parts]
    return taken[0] if len(taken) == 1 else jnp.concatenate(taken, axis=0)


def rows_of(parts, segments, halo):
    low = moved(
        ends(parts, lambda part: part[:, part.shape[1] - halo :]), segments, (0, 1, 0)
    )
    high = moved(ends(parts, lambda part: part[:, :halo]), segments, (0, -1, 0))
    return low, high


def sides_of(parts, low, high, halo):
    def side(cut):
        return jnp.concatenate([cut(low), ends(parts, cut), cut(high)], axis=1)

    return side(lambda part: part[:, :, part.shape[2] - halo :]), side(
        lambda part: part[:, :, :halo]
    )


def columns_of(left, right, segments):
    return moved(left, segments, (0, 0, 1)), moved(right, segments, (0, 0, -1))


def on_device(height, width, frames, caches, weights, biases, gains):
    sections = lax.axis_size("segment")
    place = jnp.stack(
        [lax.axis_index("row"), lax.axis_index("col"), lax.axis_index("segment")]
    ).astype(jnp.int32)
    channels = frames.shape[-1]
    kernels = weights[0].reshape((2, 3, 3, 3 * channels, channels))
    cached = caches[0].reshape((4,) + frames.shape[1:])
    halo = 2 * sections
    reach = halo - 2
    others = list(range(1, sections))
    low, high = rows_of([frames, cached], [0], halo)
    left, right = sides_of([frames, cached], low, high, halo)
    left, right = columns_of(left, right, [0])
    left, later = lax.optimization_barrier((left, cached))
    pieces = (low, high, left, right)
    low, high = rows_of([later], others, reach)
    left, right = sides_of([later], low, high, reach)
    ahead = (low, high) + columns_of(left, right, others)
    values, results = first_section(
        place, frames, cached, pieces, kernels, biases[0], gains[0], halo, height, width
    )
    values, cached = lax.optimization_barrier((values, cached))
    received = moved(values, [0], (1, 0, 0))
    known = held_part(cached, ahead, kernels, biases[0])
    halo = reach
    for step in others:
        last = step == sections - 1
        outs = later_section(
            step, place, received, known, kernels, gains[0], results,
            halo, reach - halo, last, height, width,
        )
        results = outs[-1]
        halo = halo - 2
        if not last:
            received = moved(outs[0], [step], (1, 0, 0))
    return results[None]


def solution(mesh):
    height = 16 * mesh.shape["row"]
    width = 16 * mesh.shape["col"]
    in_specs = (
        P(None, "row", "col", None),
        P("segment", None, None, "row", "col", None),
        P("segment", None, None, None, None, None, None),
        P("segment", None, None),
        P("segment", None, None),
    )
    out_specs = P("segment", None, "row", "col", None)
    return jax.shard_map(
        functools.partial(on_device, height, width),
        mesh=mesh, in_specs=in_specs, out_specs=out_specs, check_vma=False,
    )
```

```python
import functools

import jax
import jax.numpy as jnp
from jax import lax
from jax.experimental import pallas as pl
from jax.experimental.pallas import tpu as pltpu
from jax.sharding import PartitionSpec as P

PITCH = 32
CHUNK = 8
AXES = ("segment", "row", "col")


def norm_act(values, half_gain, mask):
    scale = lax.rsqrt(jnp.mean(values * values, axis=-1, keepdims=True) + 1e-06)
    half = values * scale * half_gain
    return (half + half * jnp.tanh(half)) * mask


def chunks(rows):
    return [(first, min(CHUNK, rows - first)) for first in range(0, rows, CHUNK)]


def column_mask(side, width, channels):
    col = lax.broadcasted_iota(jnp.int32, (PITCH, channels), 0) + side
    return jnp.where((col >= 0) & (col < width), 1.0, 0.0)


def cell_mask(columns, top, height, first, count):
    parts = []
    for row in range(first, first + count):
        here = top + row
        parts.append(columns * jnp.where((here >= 0) & (here < height), 1.0, 0.0))
    return jnp.concatenate(parts, axis=0)


def spread(source, start, patches, block, rows):
    channels = source.shape[-1]
    for tap in range(3):
        lane = (block * 3 + tap) * channels
        begin = start + tap
        patches[: rows * PITCH, lane : lane + channels] = source[
            begin : begin + rows * PITCH, :
        ].astype(jnp.bfloat16)


def weight_rows(kernel, tap, sides):
    empty = jnp.zeros(kernel.shape[2:], jnp.bfloat16)

    def column(taps):
        parts = [empty if t is None else kernel[t, tap] for t in taps]
        return parts[0] if len(parts) == 1 else jnp.concatenate(parts, axis=0)

    columns = [column(taps) for taps in sides]
    return columns[0] if len(columns) == 1 else jnp.concatenate(columns, axis=1)


HELD = ((0, 1), (None, 0))
OPENING = ((0, 1, 2), (None, 0, 1))
EARLY = ((2,), (1,))
LATE = ((2,),)


def convolve(patches, kernel, sides, total, first, rows):
    count = rows * PITCH
    for tap in range(3):
        begin = (first + tap) * PITCH
        total = total + jnp.dot(
            patches[begin : begin + count, :],
            weight_rows(kernel, tap, sides),
            preferred_element_type=jnp.float32,
        )
    return total


def bias_of(bias, count):
    return jnp.broadcast_to(
        jnp.concatenate([bias, bias], axis=1), (count, 2 * bias.shape[-1])
    )


def assemble(grid, source, mid, low, high, left, right):
    reach = low.shape[1]
    tile = mid.shape[1]
    for row in range(tile + 2 * reach):
        begin = row * PITCH
        if row < reach:
            body = low[source, row]
        elif row < reach + tile:
            body = mid[source, row - reach]
        else:
            body = high[source, row - reach - tile]
        grid[begin : begin + reach, :] = left[source, row].astype(jnp.float32)
        grid[begin + reach : begin + reach + tile, :] = body.astype(jnp.float32)
        grid[begin + reach + tile : begin + 2 * reach + tile, :] = right[
            source, row
        ].astype(jnp.float32)


def normed(place, margin, height, width, values_of, gain, flat, rows, span):
    channels = gain.shape[-1]
    tile = span - 2 * margin
    top = place[0] * tile - margin
    columns = column_mask(place[1] * tile - margin, width, channels)
    half_gain = 0.5 * gain
    for first, count in chunks(rows):
        keep = cell_mask(columns, top, height, first, count)
        flat[first * PITCH : (first + count) * PITCH, :] = norm_act(
            values_of(first, count), half_gain, keep
        )


def body(place, halo, height, width, g_ref, held, flat, patches, fill, hidden_of, branch_of, o_ref):
    span = o_ref.shape[0] + 4
    blocks = patches.shape[1] // (3 * held.shape[-1])

    def area(ref, first, count):
        return ref[first * PITCH : (first + count) * PITCH, :]

    normed(
        place, halo, height, width, lambda first, count: area(held, first, count),
        g_ref[0:1, :], flat, span, span,
    )
    fill(0)
    spread(flat, 0, patches, blocks - 1, span)
    normed(
        place, halo - 1, height, width, hidden_of, g_ref[1:2, :], flat, span - 2, span - 2
    )
    fill(1)
    spread(flat, 0, patches, blocks - 1, span - 2)
    for first, count in chunks(span - 4):
        offset = (first + 2) * PITCH + 2
        out = held[offset : offset + count * PITCH, :] + branch_of(first, count)
        for row in range(count):
            o_ref[first + row] = out[row * PITCH : row * PITCH + span - 4].astype(
                jnp.bfloat16
            )


def split_off(part):
    def apply(total, first, count):
        channels = part.shape[-1]
        part[first * PITCH : (first + count) * PITCH, :] = total[:, channels:]
        return total[:, :channels]

    return apply


def only_at(kernel, step):
    def run(place, *refs):
        @pl.when(place[2] == step)
        def _():
            kernel(place, *refs)

    return run


def keep_tile(o_ref, r_ref):
    tile = r_ref.shape[0]
    edge = (o_ref.shape[0] - tile) // 2
    r_ref[...] = o_ref[edge : edge + tile, edge : edge + tile, :]


def pass_on(place, step, p_ref, r_ref):
    @pl.when(place[2] != step)
    def _():
        r_ref[...] = p_ref[...]


def opening_kernel(
    halo, height, width, place, mid, low, high, left, right, w_ref, b_ref, g_ref,
    o_ref, r_ref, one_ref, two_ref, grid, flat, patches,
):
    for slot, source in enumerate((0, 2, 3, 4, 5)):
        assemble(grid.at[slot], source, mid, low, high, left, right)
    span = mid.shape[1] + 2 * halo

    def fill(conv):
        for frame in range(2):
            spread(
                grid.at[1 + 2 * conv + frame], conv * (PITCH + 1), patches, frame,
                span - 2 * conv,
            )

    def conv_of(conv, part):
        def run(first, count):
            bias = bias_of(b_ref[conv : conv + 1, :], count * PITCH)
            total = convolve(patches, w_ref.at[conv], OPENING, bias, first, count)
            return split_off(part)(total, first, count)

        return run

    body(
        place, halo, height, width, g_ref, grid.at[0], flat, patches, fill,
        conv_of(0, one_ref), conv_of(1, two_ref), o_ref,
    )
    keep_tile(o_ref, r_ref)


def nothing(conv):
    del conv


def late_of(patches, w_ref, conv, part):
    def run(first, count):
        known = part[first * PITCH : (first + count) * PITCH, :]
        return convolve(patches, w_ref.at[conv], LATE, known, first, count)

    return run


def opening_late_kernel(
    halo, height, width, place, mid, low, high, left, right, w_ref, g_ref,
    one_ref, two_ref, o_ref, r_ref, held, flat, patches,
):
    assemble(held, 1, mid, low, high, left, right)
    body(
        place, halo, height, width, g_ref, held, flat, patches, nothing,
        late_of(patches, w_ref, 0, one_ref), late_of(patches, w_ref, 1, two_ref), o_ref,
    )
    keep_tile(o_ref, r_ref)


def held_kernel(
    place, cached, low, high, left, right, w_ref, b_ref, one_ref, two_ref, grid, patches
):
    @pl.when(place[2] != 0)
    def _():
        add_held(
            cached, low, high, left, right, w_ref, b_ref, one_ref, two_ref, grid, patches
        )


def add_held(
    cached, low, high, left, right, w_ref, b_ref, one_ref, two_ref, grid, patches
):
    span = cached.shape[1] + 2 * low.shape[1]
    for frame in range(4):
        assemble(grid.at[frame], frame, cached, low, high, left, right)
    for conv, out in ((0, one_ref), (1, two_ref)):
        start = conv * (PITCH + 1)
        rows = span - 2 * conv
        for frame in range(2):
            spread(grid.at[2 * conv + frame], start, patches, frame, rows)
        for first, count in chunks(rows - 2):
            out[first * PITCH : (first + count) * PITCH, :] = convolve(
                patches, w_ref.at[conv], HELD,
                bias_of(b_ref[conv : conv + 1, :], count * PITCH), first, count,
            )


def load_rows(x_ref, held):
    span = x_ref.shape[0]
    for row in range(span):
        held[row * PITCH : row * PITCH + span, :] = x_ref[row].astype(jnp.float32)


def early_kernel(
    halo, drop, height, width, place, x_ref, known_one, known_two, w_ref, g_ref, p_ref,
    o_ref, r_ref, one_ref, two_ref, held, flat, patches,
):
    load_rows(x_ref, held)

    def conv_of(conv, known, part):
        def run(first, count):
            begin = drop * (PITCH + 1) + first * PITCH
            total = convolve(
                patches, w_ref.at[conv], EARLY, known[begin : begin + count * PITCH, :],
                first, count,
            )
            return split_off(part)(total, first, count)

        return run

    body(
        place, halo, height, width, g_ref, held, flat, patches, nothing,
        conv_of(0, known_one, one_ref), conv_of(1, known_two, two_ref), o_ref,
    )
    keep_tile(o_ref, r_ref)


def late_kernel(
    halo, height, width, place, x_ref, one_ref, two_ref, w_ref, g_ref, p_ref,
    o_ref, r_ref, held, flat, patches,
):
    load_rows(x_ref, held)
    body(
        place, halo, height, width, g_ref, held, flat, patches, nothing,
        late_of(patches, w_ref, 0, one_ref), late_of(patches, w_ref, 1, two_ref), o_ref,
    )
    keep_tile(o_ref, r_ref)


def last_kernel(
    halo, height, width, place, x_ref, one_ref, two_ref, w_ref, g_ref, p_ref, q_ref,
    r_ref, o_ref, held, flat, patches,
):
    late_kernel(
        halo, height, width, place, x_ref, one_ref, two_ref, w_ref, g_ref, p_ref,
        o_ref, r_ref.at[1], held, flat, patches,
    )


def own_or_passed(kernel, step, former, current, place, *refs):
    only_at(kernel, step)(place, *refs)
    pass_on(place, step, refs[former], refs[current])


def last_or_passed(kernel, step, former, current, place, *refs):
    refs[current][0] = refs[former + 1][...]
    only_at(kernel, step)(place, *refs)
    pass_on(place, step, refs[former], refs[current].at[1])


def pack_kernel(frames, cached, mid, low, high, sems):
    reach = low.shape[1]
    tile = frames.shape[1]
    copies = []
    for out, begin, rows in ((low, tile - reach, reach), (high, 0, reach), (mid, 0, tile)):
        for part, offset in ((frames, 0), (cached, 2)):
            copies.append(
                pltpu.make_async_copy(
                    part.at[:, pl.ds(begin, rows)],
                    out.at[pl.ds(offset, part.shape[0])],
                    sems.at[len(copies)],
                )
            )
    for copy in copies:
        copy.start()
    for copy in copies:
        copy.wait()


def sides_kernel(mid, low, high, left, right):
    reach = low.shape[1]
    tile = mid.shape[1]
    for out, begin in ((left, tile - reach), (right, 0)):
        cut = slice(begin, begin + reach)
        out[:, :reach] = low[:, :, cut, :]
        out[:, reach : reach + tile] = mid[:, :, cut, :]
        out[:, reach + tile :] = high[:, :, cut, :]


SCALARS = pl.BlockSpec(memory_space=pltpu.SMEM)
WHOLE = pl.BlockSpec(memory_space=pltpu.VMEM)


def shaped(*shape, dtype=jnp.bfloat16):
    return jax.ShapeDtypeStruct(shape, dtype)


def launch(kernel, arguments, outs, scratch, span, frames):
    channels = arguments[1].shape[-1]
    return pl.pallas_call(
        kernel,
        out_shape=outs,
        in_specs=[SCALARS] + [WHOLE] * (len(arguments) - 1),
        out_specs=[WHOLE] * len(outs),
        scratch_shapes=scratch,
        cost_estimate=pl.CostEstimate(
            flops=4 * 9 * frames * span * PITCH * channels * 2 * channels,
            bytes_accessed=2 << 20,
            transcendentals=0,
        ),
        compiler_params=pltpu.CompilerParams(vmem_limit_bytes=40 << 20),
    )(*arguments)


def room(span):
    return (span + 3) * PITCH


def scratches(span, frames, blocks, channels):
    grid = (room(span), channels)
    return [
        pltpu.VMEM(grid if frames == 1 else (frames,) + grid, jnp.float32),
        pltpu.VMEM(grid, jnp.float32),
        pltpu.VMEM((room(span), blocks * 3 * channels), jnp.bfloat16),
    ]


def parts_of(span, lanes):
    return [
        shaped((span - 2) * PITCH, lanes, dtype=jnp.float32),
        shaped((span - 4) * PITCH, lanes, dtype=jnp.float32),
    ]


def packed(frames, cached, halo):
    tile = (6,) + frames.shape[1:]
    shape = (6, halo) + frames.shape[2:]
    return pl.pallas_call(
        pack_kernel,
        out_shape=[shaped(*tile), shaped(*shape), shaped(*shape)],
        in_specs=[pl.BlockSpec(memory_space=pltpu.HBM)] * 2,
        out_specs=[WHOLE] * 3,
        scratch_shapes=[pltpu.SemaphoreType.DMA((6,))],
        compiler_params=pltpu.CompilerParams(vmem_limit_bytes=4 << 20),
    )(frames, cached)


def cut_sides(mid, low, high):
    halo = low.shape[1]
    tile, channels = mid.shape[1], mid.shape[-1]
    return pl.pallas_call(
        sides_kernel,
        out_shape=[shaped(6, tile + 2 * halo, halo, channels)] * 2,
        in_specs=[WHOLE] * 3,
        out_specs=[WHOLE] * 2,
        compiler_params=pltpu.CompilerParams(vmem_limit_bytes=8 << 20),
    )(mid, low, high)


def moved(value, segments, shift):
    sizes = [lax.axis_size(axis) for axis in AXES]
    pairs = []
    for segment in segments:
        for row in range(sizes[1]):
            for col in range(sizes[2]):
                target = (segment + shift[0], row + shift[1], col + shift[2])
                if all(0 <= t < n for t, n in zip(target, sizes)):
                    source = (segment * sizes[1] + row) * sizes[2] + col
                    place = (target[0] * sizes[1] + target[1]) * sizes[2] + target[2]
                    pairs.append((source, place))
    return lax.ppermute(value, AXES, pairs)


def ends(parts, cut):
    taken = [cut(part) for part in parts]
    return taken[0] if len(taken) == 1 else jnp.concatenate(taken, axis=0)


def rows_of(parts, segments, halo):
    low = moved(
        ends(parts, lambda part: part[:, part.shape[1] - halo :]), segments, (0, 1, 0)
    )
    high = moved(ends(parts, lambda part: part[:, :halo]), segments, (0, -1, 0))
    return low, high


def sides_of(parts, low, high, halo):
    def side(cut):
        return jnp.concatenate([cut(low), ends(parts, cut), cut(high)], axis=1)

    return side(lambda part: part[:, :, part.shape[2] - halo :]), side(
        lambda part: part[:, :, :halo]
    )


def columns_of(left, right, segments):
    return moved(left, segments, (0, 0, 1)), moved(right, segments, (0, 0, -1))


def on_device(height, width, frames, caches, weights, biases, gains):
    sections = lax.axis_size("segment")
    place = jnp.stack(
        [lax.axis_index("row"), lax.axis_index("col"), lax.axis_index("segment")]
    ).astype(jnp.int32)
    tile, channels = frames.shape[1], frames.shape[-1]
    kernels = weights[0].reshape((2, 3, 3, 3 * channels, channels))
    bias, gain = biases[0], gains[0]
    cached = caches[0].reshape((4,) + frames.shape[1:])
    halo = 2 * sections
    reach = halo - 2
    others = list(range(1, sections))
    mid, low, high = packed(frames, cached, halo)
    low, high = moved(low, [0], (0, 1, 0)), moved(high, [0], (0, -1, 0))
    left, right = cut_sides(mid, low, high)
    left, right = columns_of(left, right, [0])
    left, later = lax.optimization_barrier((left, cached))
    pieces = (mid, low, high, left, right)
    low, high = rows_of([later], others, reach)
    left, right = sides_of([later], low, high, reach)
    ahead = (low, high) + columns_of(left, right, others)

    span = tile + 2 * halo
    owned = shaped(tile, tile, channels)
    onward = shaped(span - 4, span - 4, channels)
    sent, result, one, two = launch(
        only_at(functools.partial(opening_kernel, halo, height, width), 0),
        (place,) + pieces + (kernels, bias, gain),
        [onward, owned] + parts_of(span, channels),
        scratches(span, 5, 3, channels), span, 3,
    )
    received = moved(sent, [0], (1, 0, 0))
    sent, result_late = launch(
        only_at(functools.partial(opening_late_kernel, halo, height, width), 0),
        (place,) + pieces + (kernels, gain, one, two),
        [onward, owned],
        scratches(span, 1, 1, channels), span, 1,
    )
    sent, cached = lax.optimization_barrier((sent, cached))
    received_late = moved(sent, [0], (1, 0, 0))
    span = tile + 2 * reach
    known = launch(
        held_kernel,
        (place, cached) + ahead + (kernels, bias),
        parts_of(span, 2 * channels),
        [
            pltpu.VMEM((4, room(span), channels), jnp.float32),
            pltpu.VMEM((room(span), 6 * channels), jnp.bfloat16),
        ],
        span, 2,
    )
    halo = reach
    for step in others:
        span = tile + 2 * halo
        onward = shaped(span - 4, span - 4, channels)
        sent, result, one, two = launch(
            functools.partial(
                own_or_passed,
                functools.partial(early_kernel, halo, reach - halo, height, width),
                step, 5, 7,
            ),
            (place, received, *known, kernels, gain, result),
            [onward, owned] + parts_of(span, channels),
            scratches(span, 1, 1, channels), span, 1,
        )
        if step + 1 < sections:
            received = moved(sent, [step], (1, 0, 0))
            sent, result_late = launch(
                functools.partial(
                    own_or_passed,
                    functools.partial(late_kernel, halo, height, width),
                    step, 5, 7,
                ),
                (place, received_late, one, two, kernels, gain, result_late),
                [onward, owned],
                scratches(span, 1, 1, channels), span, 1,
            )
            received_late = moved(sent, [step], (1, 0, 0))
        else:
            (result,) = launch(
                functools.partial(
                    last_or_passed,
                    functools.partial(last_kernel, halo, height, width),
                    step, 5, 7,
                ),
                (place, received_late, one, two, kernels, gain, result_late, result),
                [shaped(2, tile, tile, channels)],
                [pltpu.VMEM(onward.shape, jnp.bfloat16)] + scratches(span, 1, 1, channels),
                span, 1,
            )
        halo = halo - 2
    return result[None]


def solution(mesh):
    height = 16 * mesh.shape["row"]
    width = 16 * mesh.shape["col"]
    in_specs = (
        P(None, "row", "col", None),
        P("segment", None, None, "row", "col", None),
        P("segment", None, None, None, None, None, None),
        P("segment", None, None),
        P("segment", None, None),
    )
    out_specs = P("segment", None, "row", "col", None)
    return jax.shard_map(
        functools.partial(on_device, height, width),
        mesh=mesh, in_specs=in_specs, out_specs=out_specs, check_vma=False,
    )
```

```python
import functools

import jax
import jax.numpy as jnp
from jax import lax
from jax.experimental import pallas as pl
from jax.experimental.pallas import tpu as pltpu
from jax.sharding import PartitionSpec as P

PITCH = 32
PACK_ROOM = 58 << 20
CHUNK = 8
AXES = ("segment", "row", "col")


def norm_act(values, half_gain, mask):
    scale = lax.rsqrt(jnp.mean(values * values, axis=-1, keepdims=True) + 1e-06)
    half = values * scale * half_gain
    return (half + half * jnp.tanh(half)) * mask


def chunks(rows):
    return [(first, min(CHUNK, rows - first)) for first in range(0, rows, CHUNK)]


def column_mask(side, width, channels):
    col = lax.broadcasted_iota(jnp.int32, (PITCH, channels), 0) + side
    return jnp.where((col >= 0) & (col < width), 1.0, 0.0)


def cell_mask(columns, top, height, first, count):
    parts = []
    for row in range(first, first + count):
        here = top + row
        parts.append(columns * jnp.where((here >= 0) & (here < height), 1.0, 0.0))
    return jnp.concatenate(parts, axis=0)


def spread(source, start, patches, block, rows):
    channels = source.shape[-1]
    for tap in range(3):
        lane = (block * 3 + tap) * channels
        begin = start + tap
        patches[: rows * PITCH, lane : lane + channels] = source[
            begin : begin + rows * PITCH, :
        ].astype(jnp.bfloat16)


def weight_rows(kernel, tap, sides):
    empty = jnp.zeros(kernel.shape[2:], jnp.bfloat16)

    def column(taps):
        parts = [empty if t is None else kernel[t, tap] for t in taps]
        return parts[0] if len(parts) == 1 else jnp.concatenate(parts, axis=0)

    columns = [column(taps) for taps in sides]
    return columns[0] if len(columns) == 1 else jnp.concatenate(columns, axis=1)


HELD = ((0, 1), (None, 0))
OPENING = ((0, 1, 2), (None, 0, 1))
EARLY = ((2,), (1,))
LATE = ((2,),)


def convolve(patches, kernel, sides, total, first, rows):
    count = rows * PITCH
    for tap in range(3):
        begin = (first + tap) * PITCH
        total = total + jnp.dot(
            patches[begin : begin + count, :],
            weight_rows(kernel, tap, sides),
            preferred_element_type=jnp.float32,
        )
    return total


def bias_of(bias, count):
    return jnp.broadcast_to(
        jnp.concatenate([bias, bias], axis=1), (count, 2 * bias.shape[-1])
    )


def assemble(grid, source, mid, low, high, left, right):
    reach = low.shape[1]
    tile = mid.shape[1]
    for row in range(tile + 2 * reach):
        begin = row * PITCH
        if row < reach:
            body = low[source, row]
        elif row < reach + tile:
            body = mid[source, row - reach]
        else:
            body = high[source, row - reach - tile]
        grid[begin : begin + reach, :] = left[source, row].astype(jnp.float32)
        grid[begin + reach : begin + reach + tile, :] = body.astype(jnp.float32)
        grid[begin + reach + tile : begin + 2 * reach + tile, :] = right[
            source, row
        ].astype(jnp.float32)


def normed(margin, height, width, values_of, gain, flat, rows, span):
    channels = gain.shape[-1]
    tile = span - 2 * margin
    top = lax.axis_index("row") * tile - margin
    columns = column_mask(lax.axis_index("col") * tile - margin, width, channels)
    half_gain = 0.5 * gain
    for first, count in chunks(rows):
        keep = cell_mask(columns, top, height, first, count)
        flat[first * PITCH : (first + count) * PITCH, :] = norm_act(
            values_of(first, count), half_gain, keep
        )


def body(halo, height, width, g_ref, held, flat, patches, fill, hidden_of, branch_of, o_ref):
    span = o_ref.shape[0] + 4
    blocks = patches.shape[1] // (3 * held.shape[-1])

    def area(ref, first, count):
        return ref[first * PITCH : (first + count) * PITCH, :]

    normed(
        halo, height, width, lambda first, count: area(held, first, count),
        g_ref[0:1, :], flat, span, span,
    )
    fill(0)
    spread(flat, 0, patches, blocks - 1, span)
    normed(
        halo - 1, height, width, hidden_of, g_ref[1:2, :], flat, span - 2, span - 2
    )
    fill(1)
    spread(flat, 0, patches, blocks - 1, span - 2)
    for first, count in chunks(span - 4):
        offset = (first + 2) * PITCH + 2
        out = held[offset : offset + count * PITCH, :] + branch_of(first, count)
        for row in range(count):
            o_ref[first + row] = out[row * PITCH : row * PITCH + span - 4].astype(
                jnp.bfloat16
            )


def split_off(part):
    def apply(total, first, count):
        channels = part.shape[-1]
        part[first * PITCH : (first + count) * PITCH, :] = total[:, channels:]
        return total[:, :channels]

    return apply


def only_at(kernel, step):
    def run(*refs):
        @pl.when(lax.axis_index("segment") == step)
        def _():
            kernel(*refs)

    return run


def keep_tile(o_ref, r_ref):
    tile = r_ref.shape[0]
    edge = (o_ref.shape[0] - tile) // 2
    r_ref[...] = o_ref[edge : edge + tile, edge : edge + tile, :]


def pass_on(step, p_ref, r_ref):
    @pl.when(lax.axis_index("segment") != step)
    def _():
        r_ref[...] = p_ref[...]


def opening_kernel(
    halo, height, width, mid, low, high, left, right, w_ref, b_ref, g_ref,
    o_ref, r_ref, one_ref, two_ref, grid, flat, patches,
):
    for slot, source in enumerate((0, 2, 3, 4, 5)):
        assemble(grid.at[slot], source, mid, low, high, left, right)
    span = mid.shape[1] + 2 * halo

    def fill(conv):
        for frame in range(2):
            spread(
                grid.at[1 + 2 * conv + frame], conv * (PITCH + 1), patches, frame,
                span - 2 * conv,
            )

    def conv_of(conv, part):
        def run(first, count):
            bias = bias_of(b_ref[conv : conv + 1, :], count * PITCH)
            total = convolve(patches, w_ref.at[conv], OPENING, bias, first, count)
            return split_off(part)(total, first, count)

        return run

    body(
        halo, height, width, g_ref, grid.at[0], flat, patches, fill,
        conv_of(0, one_ref), conv_of(1, two_ref), o_ref,
    )
    keep_tile(o_ref, r_ref)


def nothing(conv):
    del conv


def late_of(patches, w_ref, conv, part):
    def run(first, count):
        known = part[first * PITCH : (first + count) * PITCH, :]
        return convolve(patches, w_ref.at[conv], LATE, known, first, count)

    return run


def opening_late_kernel(
    halo, height, width, mid, low, high, left, right, w_ref, g_ref,
    one_ref, two_ref, o_ref, r_ref, held, flat, patches,
):
    assemble(held, 1, mid, low, high, left, right)
    body(
        halo, height, width, g_ref, held, flat, patches, nothing,
        late_of(patches, w_ref, 0, one_ref), late_of(patches, w_ref, 1, two_ref), o_ref,
    )
    keep_tile(o_ref, r_ref)


def held_kernel(
    cached, low, high, left, right, w_ref, b_ref, one_ref, two_ref, grid, patches
):
    @pl.when(lax.axis_index("segment") != 0)
    def _():
        add_held(
            cached, low, high, left, right, w_ref, b_ref, one_ref, two_ref, grid, patches
        )


def add_held(
    cached, low, high, left, right, w_ref, b_ref, one_ref, two_ref, grid, patches
):
    span = cached.shape[1] + 2 * low.shape[1]
    for frame in range(4):
        assemble(grid.at[frame], frame, cached, low, high, left, right)
    for conv, out in ((0, one_ref), (1, two_ref)):
        start = conv * (PITCH + 1)
        rows = span - 2 * conv
        for frame in range(2):
            spread(grid.at[2 * conv + frame], start, patches, frame, rows)
        for first, count in chunks(rows - 2):
            out[first * PITCH : (first + count) * PITCH, :] = convolve(
                patches, w_ref.at[conv], HELD,
                bias_of(b_ref[conv : conv + 1, :], count * PITCH), first, count,
            )


def load_rows(x_ref, held):
    span = x_ref.shape[0]
    for row in range(span):
        held[row * PITCH : row * PITCH + span, :] = x_ref[row].astype(jnp.float32)


def early_kernel(
    halo, drop, height, width, x_ref, known_one, known_two, w_ref, g_ref, p_ref,
    r_ref, one_ref, two_ref, o_ref, held, flat, patches,
):
    load_rows(x_ref, held)

    def conv_of(conv, known, part):
        def run(first, count):
            begin = drop * (PITCH + 1) + first * PITCH
            total = convolve(
                patches, w_ref.at[conv], EARLY, known[begin : begin + count * PITCH, :],
                first, count,
            )
            return split_off(part)(total, first, count)

        return run

    body(
        halo, height, width, g_ref, held, flat, patches, nothing,
        conv_of(0, known_one, one_ref), conv_of(1, known_two, two_ref), o_ref,
    )
    keep_tile(o_ref, r_ref)


def late_kernel(
    halo, height, width, x_ref, one_ref, two_ref, w_ref, g_ref, p_ref,
    o_ref, r_ref, held, flat, patches,
):
    load_rows(x_ref, held)
    body(
        halo, height, width, g_ref, held, flat, patches, nothing,
        late_of(patches, w_ref, 0, one_ref), late_of(patches, w_ref, 1, two_ref), o_ref,
    )
    keep_tile(o_ref, r_ref)


def last_kernel(
    halo, height, width, x_ref, one_ref, two_ref, w_ref, g_ref, p_ref, q_ref,
    r_ref, o_ref, held, flat, patches,
):
    late_kernel(
        halo, height, width, x_ref, one_ref, two_ref, w_ref, g_ref, p_ref,
        o_ref, r_ref.at[1], held, flat, patches,
    )


def own_or_passed(kernel, step, former, current, *refs):
    only_at(kernel, step)(*refs)
    pass_on(step, refs[former], refs[current])


def last_or_passed(kernel, step, former, current, *refs):
    refs[current][0] = refs[former + 1][...]
    only_at(kernel, step)(*refs)
    pass_on(step, refs[former], refs[current].at[1])


def pack_kernel(frames, cached, low, high, sems):
    reach = low.shape[1]
    tile = frames.shape[1]
    upper, lower = pl.ds(0, reach), pl.ds(tile - reach, reach)
    copies = []
    for out, rows in (
        (low, lower), (high, upper),
    ):
        for part, offset in ((frames, 0), (cached, 2)):
            copies.append(
                pltpu.make_async_copy(
                    part.at[:, rows],
                    out.at[pl.ds(offset, part.shape[0])],
                    sems.at[len(copies)],
                )
            )
    for copy in copies:
        copy.start()
    for copy in copies:
        copy.wait()


def sides_kernel(mid, low, high, left, right):
    reach = low.shape[1]
    tile = mid.shape[1]
    for out, begin in ((left, tile - reach), (right, 0)):
        cut = slice(begin, begin + reach)
        out[:, :reach] = low[:, :, cut, :]
        out[:, reach : reach + tile] = mid[:, :, cut, :]
        out[:, reach + tile :] = high[:, :, cut, :]


WHOLE = pl.BlockSpec(memory_space=pltpu.VMEM)


def shaped(*shape, dtype=jnp.bfloat16):
    return jax.ShapeDtypeStruct(shape, dtype)


def launch(kernel, arguments, outs, scratch, span, frames):
    channels = arguments[0].shape[-1]
    return pl.pallas_call(
        kernel,
        out_shape=outs,
        in_specs=[WHOLE] * len(arguments),
        out_specs=[WHOLE] * len(outs),
        scratch_shapes=scratch,
        cost_estimate=pl.CostEstimate(
            flops=4 * 9 * frames * span * PITCH * channels * 2 * channels,
            bytes_accessed=2 << 20,
            transcendentals=0,
        ),
        compiler_params=pltpu.CompilerParams(vmem_limit_bytes=40 << 20),
    )(*arguments)


def room(span):
    return (span + 3) * PITCH


def scratches(span, frames, blocks, channels):
    grid = (room(span), channels)
    return [
        pltpu.VMEM(grid if frames == 1 else (frames,) + grid, jnp.float32),
        pltpu.VMEM(grid, jnp.float32),
        pltpu.VMEM((room(span), blocks * 3 * channels), jnp.bfloat16),
    ]


def parts_of(span, lanes):
    return [
        shaped((span - 2) * PITCH, lanes, dtype=jnp.float32),
        shaped((span - 4) * PITCH, lanes, dtype=jnp.float32),
    ]


def packed(frames, cached, halo):
    shape = (6, halo) + frames.shape[2:]
    return pl.pallas_call(
        pack_kernel,
        out_shape=[shaped(*shape)] * 2,
        in_specs=[pl.BlockSpec(memory_space=pltpu.HBM)] * 2,
        out_specs=[pl.BlockSpec(memory_space=pltpu.HBM)] * 2,
        scratch_shapes=[pltpu.SemaphoreType.DMA((4,))],
        compiler_params=pltpu.CompilerParams(vmem_limit_bytes=PACK_ROOM),
    )(frames, cached)


def join_kernel(frames, cached, mid):
    mid[0:2] = frames[...]
    mid[2:6] = cached[...]


def joined(frames, cached):
    return pl.pallas_call(
        join_kernel,
        out_shape=shaped(6, *frames.shape[1:]),
        in_specs=[WHOLE] * 2,
        out_specs=WHOLE,
        cost_estimate=pl.CostEstimate(flops=1 << 28, bytes_accessed=1 << 20, transcendentals=0),
        compiler_params=pltpu.CompilerParams(vmem_limit_bytes=4 << 20),
    )(frames, cached)


def cut_sides(mid, low, high):
    halo = low.shape[1]
    tile, channels = mid.shape[1], mid.shape[-1]
    return pl.pallas_call(
        sides_kernel,
        out_shape=[shaped(6, tile + 2 * halo, halo, channels)] * 2,
        in_specs=[WHOLE] * 3,
        out_specs=[WHOLE] * 2,
        compiler_params=pltpu.CompilerParams(vmem_limit_bytes=8 << 20),
    )(mid, low, high)


def moved(value, segments, shift):
    sizes = [lax.axis_size(axis) for axis in AXES]
    pairs = []
    for segment in segments:
        for row in range(sizes[1]):
            for col in range(sizes[2]):
                target = (segment + shift[0], row + shift[1], col + shift[2])
                if all(0 <= t < n for t, n in zip(target, sizes)):
                    source = (segment * sizes[1] + row) * sizes[2] + col
                    place = (target[0] * sizes[1] + target[1]) * sizes[2] + target[2]
                    pairs.append((source, place))
    return lax.ppermute(value, AXES, pairs)


def ends(parts, cut):
    taken = [cut(part) for part in parts]
    return taken[0] if len(taken) == 1 else jnp.concatenate(taken, axis=0)


def rows_of(parts, segments, halo):
    low = moved(
        ends(parts, lambda part: part[:, part.shape[1] - halo :]), segments, (0, 1, 0)
    )
    high = moved(ends(parts, lambda part: part[:, :halo]), segments, (0, -1, 0))
    return low, high


def sides_of(parts, low, high, halo):
    def side(cut):
        return jnp.concatenate([cut(low), ends(parts, cut), cut(high)], axis=1)

    return side(lambda part: part[:, :, part.shape[2] - halo :]), side(
        lambda part: part[:, :, :halo]
    )


def columns_of(left, right, segments):
    return moved(left, segments, (0, 0, 1)), moved(right, segments, (0, 0, -1))


def on_device(height, width, frames, caches, weights, biases, gains):
    sections = lax.axis_size("segment")
    tile, channels = frames.shape[1], frames.shape[-1]
    kernels = weights[0].reshape((2, 3, 3, 3 * channels, channels))
    bias, gain = biases[0], gains[0]
    cached = caches[0].reshape((4,) + frames.shape[1:])
    halo = 2 * sections
    reach = halo - 2
    others = list(range(1, sections))
    low, high = packed(frames, cached, halo)
    mid = joined(frames, cached)
    low, high = moved(low, [0], (0, 1, 0)), moved(high, [0], (0, -1, 0))
    left, right = cut_sides(mid, low, high)
    left, right = columns_of(left, right, [0])
    left, later = lax.optimization_barrier((left, mid))
    later = later[2:]
    pieces = (mid, low, high, left, right)
    low, high = rows_of([later], others, reach)
    left, right = sides_of([later], low, high, reach)
    ahead = (low, high) + columns_of(left, right, others)

    span = tile + 2 * halo
    owned = shaped(tile, tile, channels)
    onward = shaped(span - 4, span - 4, channels)
    sent, result, one, two = launch(
        only_at(functools.partial(opening_kernel, halo, height, width), 0),
        pieces + (kernels, bias, gain),
        [onward, owned] + parts_of(span, channels),
        scratches(span, 5, 3, channels), span, 3,
    )
    received = moved(sent, [0], (1, 0, 0))
    sent, result_late = launch(
        only_at(functools.partial(opening_late_kernel, halo, height, width), 0),
        pieces + (kernels, gain, one, two),
        [onward, owned],
        scratches(span, 1, 1, channels), span, 1,
    )
    sent, cached = lax.optimization_barrier((sent, cached))
    received_late = moved(sent, [0], (1, 0, 0))
    span = tile + 2 * reach
    known = launch(
        held_kernel,
        (cached,) + ahead + (kernels, bias),
        parts_of(span, 2 * channels),
        [
            pltpu.VMEM((4, room(span), channels), jnp.float32),
            pltpu.VMEM((room(span), 6 * channels), jnp.bfloat16),
        ],
        span, 2,
    )
    halo = reach
    for step in others:
        span = tile + 2 * halo
        onward = shaped(span - 4, span - 4, channels)
        last = step + 1 == sections
        kernel = functools.partial(early_kernel, halo, reach - halo, height, width)
        outs = [owned] + parts_of(span, channels)
        scratch = scratches(span, 1, 1, channels)
        if last:
            scratch = [pltpu.VMEM(onward.shape, jnp.bfloat16)] + scratch
        else:
            outs = outs + [onward]
        result, one, two, *sent = launch(
            functools.partial(own_or_passed, kernel, step, 5, 6),
            (received, *known, kernels, gain, result),
            outs, scratch, span, 1,
        )
        if last:
            (result,) = launch(
                functools.partial(
                    last_or_passed,
                    functools.partial(last_kernel, halo, height, width),
                    step, 5, 7,
                ),
                (received_late, one, two, kernels, gain, result_late, result),
                [shaped(2, tile, tile, channels)],
                [pltpu.VMEM(onward.shape, jnp.bfloat16)] + scratches(span, 1, 1, channels),
                span, 1,
            )
        else:
            received = moved(sent[0], [step], (1, 0, 0))
            sent, result_late = launch(
                functools.partial(
                    own_or_passed,
                    functools.partial(late_kernel, halo, height, width),
                    step, 5, 7,
                ),
                (received_late, one, two, kernels, gain, result_late),
                [onward, owned],
                scratches(span, 1, 1, channels), span, 1,
            )
            received_late = moved(sent, [step], (1, 0, 0))
        halo = halo - 2
    return result[None]


def solution(mesh):
    height = 16 * mesh.shape["row"]
    width = 16 * mesh.shape["col"]
    in_specs = (
        P(None, "row", "col", None),
        P("segment", None, None, "row", "col", None),
        P("segment", None, None, None, None, None, None),
        P("segment", None, None),
        P("segment", None, None),
    )
    out_specs = P("segment", None, "row", "col", None)
    return jax.shard_map(
        functools.partial(on_device, height, width),
        mesh=mesh, in_specs=in_specs, out_specs=out_specs, check_vma=False,
    )
```

```python
import functools

import jax
import jax.numpy as jnp
from jax import lax
from jax.experimental import pallas as pl
from jax.experimental.pallas import tpu as pltpu
from jax.sharding import PartitionSpec as P

PITCH = 32
PACK_ROOM = 4 << 20
CHUNK = 8
AXES = ("segment", "row", "col")


def norm_act(values, half_gain, mask):
    scale = lax.rsqrt(jnp.mean(values * values, axis=-1, keepdims=True) + 1e-06)
    half = values * scale * half_gain
    return (half + half * jnp.tanh(half)) * mask


def chunks(rows):
    return [(first, min(CHUNK, rows - first)) for first in range(0, rows, CHUNK)]


def column_mask(side, width, channels):
    col = lax.broadcasted_iota(jnp.int32, (PITCH, channels), 0) + side
    return jnp.where((col >= 0) & (col < width), 1.0, 0.0)


def cell_mask(columns, top, height, first, count):
    parts = []
    for row in range(first, first + count):
        here = top + row
        parts.append(columns * jnp.where((here >= 0) & (here < height), 1.0, 0.0))
    return jnp.concatenate(parts, axis=0)


def spread(source, start, patches, block, rows):
    channels = source.shape[-1]
    for tap in range(3):
        lane = (block * 3 + tap) * channels
        begin = start + tap
        patches[: rows * PITCH, lane : lane + channels] = source[
            begin : begin + rows * PITCH, :
        ].astype(jnp.bfloat16)


def weight_rows(kernel, tap, sides):
    empty = jnp.zeros(kernel.shape[2:], jnp.bfloat16)

    def column(taps):
        parts = [empty if t is None else kernel[t, tap] for t in taps]
        return parts[0] if len(parts) == 1 else jnp.concatenate(parts, axis=0)

    columns = [column(taps) for taps in sides]
    return columns[0] if len(columns) == 1 else jnp.concatenate(columns, axis=1)


HELD = ((0, 1), (None, 0))
OPENING = ((0, 1, 2), (None, 0, 1))
EARLY = ((2,), (1,))
LATE = ((2,),)


def convolve(patches, kernel, sides, total, first, rows):
    count = rows * PITCH
    for tap in range(3):
        begin = (first + tap) * PITCH
        total = total + jnp.dot(
            patches[begin : begin + count, :],
            weight_rows(kernel, tap, sides),
            preferred_element_type=jnp.float32,
        )
    return total


def bias_of(bias, count):
    return jnp.broadcast_to(
        jnp.concatenate([bias, bias], axis=1), (count, 2 * bias.shape[-1])
    )


def assemble(grid, source, mid, low, high, left, right):
    reach = low.shape[1]
    tile = mid.shape[1]
    for row in range(tile + 2 * reach):
        begin = row * PITCH
        if row < reach:
            body = low[source, row]
        elif row < reach + tile:
            body = mid[source, row - reach]
        else:
            body = high[source, row - reach - tile]
        grid[begin : begin + reach, :] = left[source, row].astype(jnp.float32)
        grid[begin + reach : begin + reach + tile, :] = body.astype(jnp.float32)
        grid[begin + reach + tile : begin + 2 * reach + tile, :] = right[
            source, row
        ].astype(jnp.float32)


def normed(margin, height, width, values_of, gain, flat, rows, span):
    channels = gain.shape[-1]
    tile = span - 2 * margin
    top = lax.axis_index("row") * tile - margin
    columns = column_mask(lax.axis_index("col") * tile - margin, width, channels)
    half_gain = 0.5 * gain
    for first, count in chunks(rows):
        keep = cell_mask(columns, top, height, first, count)
        flat[first * PITCH : (first + count) * PITCH, :] = norm_act(
            values_of(first, count), half_gain, keep
        )


def body(halo, height, width, g_ref, held, flat, patches, fill, hidden_of, branch_of, o_ref):
    span = o_ref.shape[0] + 4
    blocks = patches.shape[1] // (3 * held.shape[-1])

    def area(ref, first, count):
        return ref[first * PITCH : (first + count) * PITCH, :]

    normed(
        halo, height, width, lambda first, count: area(held, first, count),
        g_ref[0:1, :], flat, span, span,
    )
    fill(0)
    spread(flat, 0, patches, blocks - 1, span)
    normed(
        halo - 1, height, width, hidden_of, g_ref[1:2, :], flat, span - 2, span - 2
    )
    fill(1)
    spread(flat, 0, patches, blocks - 1, span - 2)
    for first, count in chunks(span - 4):
        offset = (first + 2) * PITCH + 2
        out = held[offset : offset + count * PITCH, :] + branch_of(first, count)
        for row in range(count):
            o_ref[first + row] = out[row * PITCH : row * PITCH + span - 4].astype(
                jnp.bfloat16
            )


def split_off(part):
    def apply(total, first, count):
        channels = part.shape[-1]
        part[first * PITCH : (first + count) * PITCH, :] = total[:, channels:]
        return total[:, :channels]

    return apply


def only_at(kernel, step):
    def run(*refs):
        @pl.when(lax.axis_index("segment") == step)
        def _():
            kernel(*refs)

    return run


def keep_tile(o_ref, r_ref):
    tile = r_ref.shape[0]
    edge = (o_ref.shape[0] - tile) // 2
    r_ref[...] = o_ref[edge : edge + tile, edge : edge + tile, :]


def pass_on(step, p_ref, r_ref):
    @pl.when(lax.axis_index("segment") != step)
    def _():
        r_ref[...] = p_ref[...]


def opening_kernel(
    halo, height, width, mid, low, high, left, right, w_ref, b_ref, g_ref,
    o_ref, r_ref, one_ref, two_ref, grid, flat, patches,
):
    for slot, source in enumerate((0, 2, 3, 4, 5)):
        assemble(grid.at[slot], source, mid, low, high, left, right)
    span = mid.shape[1] + 2 * halo

    def fill(conv):
        for frame in range(2):
            spread(
                grid.at[1 + 2 * conv + frame], conv * (PITCH + 1), patches, frame,
                span - 2 * conv,
            )

    def conv_of(conv, part):
        def run(first, count):
            bias = bias_of(b_ref[conv : conv + 1, :], count * PITCH)
            total = convolve(patches, w_ref.at[conv], OPENING, bias, first, count)
            return split_off(part)(total, first, count)

        return run

    body(
        halo, height, width, g_ref, grid.at[0], flat, patches, fill,
        conv_of(0, one_ref), conv_of(1, two_ref), o_ref,
    )
    keep_tile(o_ref, r_ref)


def nothing(conv):
    del conv


def late_of(patches, w_ref, conv, part):
    def run(first, count):
        known = part[first * PITCH : (first + count) * PITCH, :]
        return convolve(patches, w_ref.at[conv], LATE, known, first, count)

    return run


def opening_late_kernel(
    halo, height, width, mid, low, high, left, right, w_ref, g_ref,
    one_ref, two_ref, o_ref, r_ref, held, flat, patches,
):
    assemble(held, 1, mid, low, high, left, right)
    body(
        halo, height, width, g_ref, held, flat, patches, nothing,
        late_of(patches, w_ref, 0, one_ref), late_of(patches, w_ref, 1, two_ref), o_ref,
    )
    keep_tile(o_ref, r_ref)


def held_kernel(
    cached, low, high, left, right, w_ref, b_ref, one_ref, two_ref, grid, patches
):
    @pl.when(lax.axis_index("segment") != 0)
    def _():
        add_held(
            cached, low, high, left, right, w_ref, b_ref, one_ref, two_ref, grid, patches
        )


def add_held(
    cached, low, high, left, right, w_ref, b_ref, one_ref, two_ref, grid, patches
):
    span = cached.shape[1] + 2 * low.shape[1]
    for frame in range(4):
        assemble(grid.at[frame], frame, cached, low, high, left, right)
    for conv, out in ((0, one_ref), (1, two_ref)):
        start = conv * (PITCH + 1)
        rows = span - 2 * conv
        for frame in range(2):
            spread(grid.at[2 * conv + frame], start, patches, frame, rows)
        for first, count in chunks(rows - 2):
            out[first * PITCH : (first + count) * PITCH, :] = convolve(
                patches, w_ref.at[conv], HELD,
                bias_of(b_ref[conv : conv + 1, :], count * PITCH), first, count,
            )


def load_rows(x_ref, held):
    span = x_ref.shape[0]
    for row in range(span):
        held[row * PITCH : row * PITCH + span, :] = x_ref[row].astype(jnp.float32)


def early_kernel(
    halo, drop, height, width, x_ref, known_one, known_two, w_ref, g_ref, p_ref,
    r_ref, one_ref, two_ref, o_ref, held, flat, patches,
):
    load_rows(x_ref, held)

    def conv_of(conv, known, part):
        def run(first, count):
            begin = drop * (PITCH + 1) + first * PITCH
            total = convolve(
                patches, w_ref.at[conv], EARLY, known[begin : begin + count * PITCH, :],
                first, count,
            )
            return split_off(part)(total, first, count)

        return run

    body(
        halo, height, width, g_ref, held, flat, patches, nothing,
        conv_of(0, known_one, one_ref), conv_of(1, known_two, two_ref), o_ref,
    )
    keep_tile(o_ref, r_ref)


def late_kernel(
    halo, height, width, x_ref, one_ref, two_ref, w_ref, g_ref, p_ref,
    o_ref, r_ref, held, flat, patches,
):
    load_rows(x_ref, held)
    body(
        halo, height, width, g_ref, held, flat, patches, nothing,
        late_of(patches, w_ref, 0, one_ref), late_of(patches, w_ref, 1, two_ref), o_ref,
    )
    keep_tile(o_ref, r_ref)


def last_kernel(
    halo, height, width, x_ref, one_ref, two_ref, w_ref, g_ref, p_ref, q_ref,
    r_ref, o_ref, held, flat, patches,
):
    late_kernel(
        halo, height, width, x_ref, one_ref, two_ref, w_ref, g_ref, p_ref,
        o_ref, r_ref.at[1], held, flat, patches,
    )


def own_or_passed(kernel, step, former, current, *refs):
    only_at(kernel, step)(*refs)
    pass_on(step, refs[former], refs[current])


def last_or_passed(kernel, step, former, current, *refs):
    refs[current][0] = refs[former + 1][...]
    only_at(kernel, step)(*refs)
    pass_on(step, refs[former], refs[current].at[1])


def pack_kernel(frames, cached, mid, low, high, sems):
    reach = low.shape[1]
    tile = frames.shape[1]
    upper, lower, every = pl.ds(0, reach), pl.ds(tile - reach, reach), pl.ds(0, tile)
    copies = []
    for out, rows in (
        (low, lower), (high, upper), (mid, every),
    ):
        for part, offset in ((frames, 0), (cached, 2)):
            copies.append(
                pltpu.make_async_copy(
                    part.at[:, rows],
                    out.at[pl.ds(offset, part.shape[0])],
                    sems.at[len(copies)],
                )
            )
    for copy in copies:
        copy.start()
    for copy in copies:
        copy.wait()


def sides_kernel(mid, low, high, left, right):
    reach = low.shape[1]
    tile = mid.shape[1]
    for out, begin in ((left, tile - reach), (right, 0)):
        cut = slice(begin, begin + reach)
        out[:, :reach] = low[:, :, cut, :]
        out[:, reach : reach + tile] = mid[:, :, cut, :]
        out[:, reach + tile :] = high[:, :, cut, :]


WHOLE = pl.BlockSpec(memory_space=pltpu.VMEM)


def shaped(*shape, dtype=jnp.bfloat16):
    return jax.ShapeDtypeStruct(shape, dtype)


def launch(kernel, arguments, outs, scratch, span, frames):
    channels = arguments[0].shape[-1]
    return pl.pallas_call(
        kernel,
        out_shape=outs,
        in_specs=[WHOLE] * len(arguments),
        out_specs=[WHOLE] * len(outs),
        scratch_shapes=scratch,
        cost_estimate=pl.CostEstimate(
            flops=4 * 9 * frames * span * PITCH * channels * 2 * channels,
            bytes_accessed=2 << 20,
            transcendentals=0,
        ),
        compiler_params=pltpu.CompilerParams(vmem_limit_bytes=40 << 20),
    )(*arguments)


def room(span):
    return (span + 3) * PITCH


def scratches(span, frames, blocks, channels):
    grid = (room(span), channels)
    return [
        pltpu.VMEM(grid if frames == 1 else (frames,) + grid, jnp.float32),
        pltpu.VMEM(grid, jnp.float32),
        pltpu.VMEM((room(span), blocks * 3 * channels), jnp.bfloat16),
    ]


def parts_of(span, lanes):
    return [
        shaped((span - 2) * PITCH, lanes, dtype=jnp.float32),
        shaped((span - 4) * PITCH, lanes, dtype=jnp.float32),
    ]


def packed(frames, cached, halo):
    tile = (6,) + frames.shape[1:]
    shape = (6, halo) + frames.shape[2:]
    return pl.pallas_call(
        pack_kernel,
        out_shape=[shaped(*tile), shaped(*shape), shaped(*shape)],
        in_specs=[pl.BlockSpec(memory_space=pltpu.HBM)] * 2,
        out_specs=[WHOLE] * 3,
        scratch_shapes=[pltpu.SemaphoreType.DMA((6,))],
        compiler_params=pltpu.CompilerParams(vmem_limit_bytes=PACK_ROOM),
    )(frames, cached)


def cut_sides(mid, low, high):
    halo = low.shape[1]
    tile, channels = mid.shape[1], mid.shape[-1]
    return pl.pallas_call(
        sides_kernel,
        out_shape=[shaped(6, tile + 2 * halo, halo, channels)] * 2,
        in_specs=[WHOLE] * 3,
        out_specs=[WHOLE] * 2,
        compiler_params=pltpu.CompilerParams(vmem_limit_bytes=8 << 20),
    )(mid, low, high)


def moved(value, segments, shift):
    sizes = [lax.axis_size(axis) for axis in AXES]
    pairs = []
    for segment in segments:
        for row in range(sizes[1]):
            for col in range(sizes[2]):
                target = (segment + shift[0], row + shift[1], col + shift[2])
                if all(0 <= t < n for t, n in zip(target, sizes)):
                    source = (segment * sizes[1] + row) * sizes[2] + col
                    place = (target[0] * sizes[1] + target[1]) * sizes[2] + target[2]
                    pairs.append((source, place))
    return lax.ppermute(value, AXES, pairs)


def ends(parts, cut):
    taken = [cut(part) for part in parts]
    return taken[0] if len(taken) == 1 else jnp.concatenate(taken, axis=0)


def rows_of(parts, segments, halo):
    low = moved(
        ends(parts, lambda part: part[:, part.shape[1] - halo :]), segments, (0, 1, 0)
    )
    high = moved(ends(parts, lambda part: part[:, :halo]), segments, (0, -1, 0))
    return low, high


def sides_of(parts, low, high, halo):
    def side(cut):
        return jnp.concatenate([cut(low), ends(parts, cut), cut(high)], axis=1)

    return side(lambda part: part[:, :, part.shape[2] - halo :]), side(
        lambda part: part[:, :, :halo]
    )


def columns_of(left, right, segments):
    return moved(left, segments, (0, 0, 1)), moved(right, segments, (0, 0, -1))


def on_device(height, width, frames, caches, weights, biases, gains):
    sections = lax.axis_size("segment")
    tile, channels = frames.shape[1], frames.shape[-1]
    kernels = weights[0].reshape((2, 3, 3, 3 * channels, channels))
    bias, gain = biases[0], gains[0]
    cached = caches[0].reshape((4,) + frames.shape[1:])
    halo = 2 * sections
    reach = halo - 2
    others = list(range(1, sections))
    mid, low, high = packed(frames, cached, halo)
    low, high = moved(low, [0], (0, 1, 0)), moved(high, [0], (0, -1, 0))
    left, right = cut_sides(mid, low, high)
    left, right = columns_of(left, right, [0])
    left, later = lax.optimization_barrier((left, mid))
    later = later[2:]
    pieces = (mid, low, high, left, right)
    low, high = rows_of([later], others, reach)
    left, right = sides_of([later], low, high, reach)
    ahead = (low, high) + columns_of(left, right, others)

    span = tile + 2 * halo
    owned = shaped(tile, tile, channels)
    onward = shaped(span - 4, span - 4, channels)
    sent, result, one, two = launch(
        only_at(functools.partial(opening_kernel, halo, height, width), 0),
        pieces + (kernels, bias, gain),
        [onward, owned] + parts_of(span, channels),
        scratches(span, 5, 3, channels), span, 3,
    )
    received = moved(sent, [0], (1, 0, 0))
    sent, result_late = launch(
        only_at(functools.partial(opening_late_kernel, halo, height, width), 0),
        pieces + (kernels, gain, one, two),
        [onward, owned],
        scratches(span, 1, 1, channels), span, 1,
    )
    sent, cached = lax.optimization_barrier((sent, cached))
    received_late = moved(sent, [0], (1, 0, 0))
    span = tile + 2 * reach
    known = launch(
        held_kernel,
        (cached,) + ahead + (kernels, bias),
        parts_of(span, 2 * channels),
        [
            pltpu.VMEM((4, room(span), channels), jnp.float32),
            pltpu.VMEM((room(span), 6 * channels), jnp.bfloat16),
        ],
        span, 2,
    )
    halo = reach
    for step in others:
        span = tile + 2 * halo
        onward = shaped(span - 4, span - 4, channels)
        last = step + 1 == sections
        kernel = functools.partial(early_kernel, halo, reach - halo, height, width)
        outs = [owned] + parts_of(span, channels)
        scratch = scratches(span, 1, 1, channels)
        if last:
            scratch = [pltpu.VMEM(onward.shape, jnp.bfloat16)] + scratch
        else:
            outs = outs + [onward]
        result, one, two, *sent = launch(
            functools.partial(own_or_passed, kernel, step, 5, 6),
            (received, *known, kernels, gain, result),
            outs, scratch, span, 1,
        )
        if last:
            (result,) = launch(
                functools.partial(
                    last_or_passed,
                    functools.partial(last_kernel, halo, height, width),
                    step, 5, 7,
                ),
                (received_late, one, two, kernels, gain, result_late, result),
                [shaped(2, tile, tile, channels)],
                [pltpu.VMEM(onward.shape, jnp.bfloat16)] + scratches(span, 1, 1, channels),
                span, 1,
            )
        else:
            received = moved(sent[0], [step], (1, 0, 0))
            sent, result_late = launch(
                functools.partial(
                    own_or_passed,
                    functools.partial(late_kernel, halo, height, width),
                    step, 5, 7,
                ),
                (received_late, one, two, kernels, gain, result_late),
                [onward, owned],
                scratches(span, 1, 1, channels), span, 1,
            )
            received_late = moved(sent, [step], (1, 0, 0))
        halo = halo - 2
    return result[None]


def solution(mesh):
    height = 16 * mesh.shape["row"]
    width = 16 * mesh.shape["col"]
    in_specs = (
        P(None, "row", "col", None),
        P("segment", None, None, "row", "col", None),
        P("segment", None, None, None, None, None, None),
        P("segment", None, None),
        P("segment", None, None),
    )
    out_specs = P("segment", None, "row", "col", None)
    return jax.shard_map(
        functools.partial(on_device, height, width),
        mesh=mesh, in_specs=in_specs, out_specs=out_specs, check_vma=False,
    )
```

```python
import functools

import jax
import jax.numpy as jnp
from jax import lax
from jax.experimental import pallas as pl
from jax.experimental.pallas import tpu as pltpu
from jax.sharding import PartitionSpec as P

PITCH = 32
PACK_ROOM = 4 << 20
CHUNK = 8
AXES = ("segment", "row", "col")


def norm_act(values, half_gain, mask):
    scale = lax.rsqrt(jnp.mean(values * values, axis=-1, keepdims=True) + 1e-06)
    half = values * scale * half_gain
    return (half + half * jnp.tanh(half)) * mask


def chunks(rows, size=CHUNK):
    return [(first, min(size, rows - first)) for first in range(0, rows, size)]


def column_mask(side, width, channels):
    col = lax.broadcasted_iota(jnp.int32, (PITCH, channels), 0) + side
    return jnp.where((col >= 0) & (col < width), 1.0, 0.0)


def cell_mask(columns, top, height, first, count):
    parts = []
    for row in range(first, first + count):
        here = top + row
        parts.append(columns * jnp.where((here >= 0) & (here < height), 1.0, 0.0))
    return jnp.concatenate(parts, axis=0)


def spread(source, start, patches, block, rows):
    channels = source.shape[-1]
    for tap in range(3):
        lane = (block * 3 + tap) * channels
        begin = start + tap
        patches[: rows * PITCH, lane : lane + channels] = source[
            begin : begin + rows * PITCH, :
        ].astype(jnp.bfloat16)


def weight_rows(kernel, tap, sides):
    empty = jnp.zeros(kernel.shape[2:], jnp.bfloat16)

    def column(taps):
        parts = [empty if t is None else kernel[t, tap] for t in taps]
        return parts[0] if len(parts) == 1 else jnp.concatenate(parts, axis=0)

    columns = [column(taps) for taps in sides]
    return columns[0] if len(columns) == 1 else jnp.concatenate(columns, axis=1)


HELD = ((0, 1), (None, 0))
OPENING = ((0, 1, 2), (None, 0, 1))
EARLY = ((2,), (1,))
LATE = ((2,),)


def convolve(patches, kernel, sides, total, first, rows):
    count = rows * PITCH
    starts = [(first + tap) * PITCH for tap in range(3)]
    cells = jnp.concatenate([patches[begin : begin + count, :] for begin in starts], axis=1)
    weight = jnp.concatenate([weight_rows(kernel, tap, sides) for tap in range(3)], axis=0)
    return total + jnp.dot(cells, weight, preferred_element_type=jnp.float32)


def bias_of(bias, count):
    return jnp.broadcast_to(
        jnp.concatenate([bias, bias], axis=1), (count, 2 * bias.shape[-1])
    )


def assemble(grid, source, mid, low, high, left, right):
    reach = low.shape[1]
    tile = mid.shape[1]
    for row in range(tile + 2 * reach):
        begin = row * PITCH
        if row < reach:
            body = low[source, row]
        elif row < reach + tile:
            body = mid[source, row - reach]
        else:
            body = high[source, row - reach - tile]
        grid[begin : begin + reach, :] = left[source, row].astype(jnp.float32)
        grid[begin + reach : begin + reach + tile, :] = body.astype(jnp.float32)
        grid[begin + reach + tile : begin + 2 * reach + tile, :] = right[
            source, row
        ].astype(jnp.float32)


def normed(margin, height, width, values_of, gain, flat, rows, span, size):
    channels = gain.shape[-1]
    tile = span - 2 * margin
    top = lax.axis_index("row") * tile - margin
    columns = column_mask(lax.axis_index("col") * tile - margin, width, channels)
    half_gain = 0.5 * gain
    for first, count in chunks(rows, size):
        keep = cell_mask(columns, top, height, first, count)
        flat[first * PITCH : (first + count) * PITCH, :] = norm_act(
            values_of(first, count), half_gain, keep
        )


def body(halo, height, width, g_ref, held, flat, patches, fill, hidden_of, branch_of, o_ref, size):
    span = o_ref.shape[0] + 4
    blocks = patches.shape[1] // (3 * held.shape[-1])

    def area(ref, first, count):
        return ref[first * PITCH : (first + count) * PITCH, :]

    normed(
        halo, height, width, lambda first, count: area(held, first, count),
        g_ref[0:1, :], flat, span, span, size,
    )
    fill(0)
    spread(flat, 0, patches, blocks - 1, span)
    normed(
        halo - 1, height, width, hidden_of, g_ref[1:2, :], flat, span - 2, span - 2, size
    )
    fill(1)
    spread(flat, 0, patches, blocks - 1, span - 2)
    for first, count in chunks(span - 4, size):
        offset = (first + 2) * PITCH + 2
        out = held[offset : offset + count * PITCH, :] + branch_of(first, count)
        for row in range(count):
            o_ref[first + row] = out[row * PITCH : row * PITCH + span - 4].astype(
                jnp.bfloat16
            )


def split_off(part):
    def apply(total, first, count):
        channels = part.shape[-1]
        part[first * PITCH : (first + count) * PITCH, :] = total[:, channels:]
        return total[:, :channels]

    return apply


def only_at(kernel, step):
    def run(*refs):
        @pl.when(lax.axis_index("segment") == step)
        def _():
            kernel(*refs)

    return run


def keep_tile(o_ref, r_ref):
    tile = r_ref.shape[0]
    edge = (o_ref.shape[0] - tile) // 2
    r_ref[...] = o_ref[edge : edge + tile, edge : edge + tile, :]


def pass_on(step, p_ref, r_ref):
    @pl.when(lax.axis_index("segment") != step)
    def _():
        r_ref[...] = p_ref[...]


def opening_kernel(
    halo, height, width, mid, low, high, left, right, w_ref, b_ref, g_ref,
    o_ref, r_ref, one_ref, two_ref, grid, flat, patches,
):
    for slot, source in enumerate((0, 2, 3, 4, 5)):
        assemble(grid.at[slot], source, mid, low, high, left, right)
    span = mid.shape[1] + 2 * halo

    def fill(conv):
        for frame in range(2):
            spread(
                grid.at[1 + 2 * conv + frame], conv * (PITCH + 1), patches, frame,
                span - 2 * conv,
            )

    def conv_of(conv, part):
        def run(first, count):
            bias = bias_of(b_ref[conv : conv + 1, :], count * PITCH)
            total = convolve(patches, w_ref.at[conv], OPENING, bias, first, count)
            return split_off(part)(total, first, count)

        return run

    body(
        halo, height, width, g_ref, grid.at[0], flat, patches, fill,
        conv_of(0, one_ref), conv_of(1, two_ref), o_ref, 10,
    )
    keep_tile(o_ref, r_ref)


def nothing(conv):
    del conv


def late_of(patches, w_ref, conv, part):
    def run(first, count):
        known = part[first * PITCH : (first + count) * PITCH, :]
        return convolve(patches, w_ref.at[conv], LATE, known, first, count)

    return run


def opening_late_kernel(
    halo, height, width, mid, low, high, left, right, w_ref, g_ref,
    one_ref, two_ref, o_ref, r_ref, held, flat, patches,
):
    assemble(held, 1, mid, low, high, left, right)
    body(
        halo, height, width, g_ref, held, flat, patches, nothing,
        late_of(patches, w_ref, 0, one_ref), late_of(patches, w_ref, 1, two_ref), o_ref, 4,
    )
    keep_tile(o_ref, r_ref)


def held_kernel(
    cached, low, high, left, right, w_ref, b_ref, one_ref, two_ref, grid, patches
):
    @pl.when(lax.axis_index("segment") != 0)
    def _():
        add_held(
            cached, low, high, left, right, w_ref, b_ref, one_ref, two_ref, grid, patches
        )


def add_held(
    cached, low, high, left, right, w_ref, b_ref, one_ref, two_ref, grid, patches
):
    span = cached.shape[1] + 2 * low.shape[1]
    for frame in range(4):
        assemble(grid.at[frame], frame, cached, low, high, left, right)
    for conv, out in ((0, one_ref), (1, two_ref)):
        start = conv * (PITCH + 1)
        rows = span - 2 * conv
        for frame in range(2):
            spread(grid.at[2 * conv + frame], start, patches, frame, rows)
        for first, count in chunks(rows - 2):
            out[first * PITCH : (first + count) * PITCH, :] = convolve(
                patches, w_ref.at[conv], HELD,
                bias_of(b_ref[conv : conv + 1, :], count * PITCH), first, count,
            )


def load_rows(x_ref, held):
    span = x_ref.shape[0]
    for row in range(span):
        held[row * PITCH : row * PITCH + span, :] = x_ref[row].astype(jnp.float32)


def early_kernel(
    halo, drop, height, width, x_ref, known_one, known_two, w_ref, g_ref, p_ref,
    r_ref, one_ref, two_ref, o_ref, held, flat, patches,
):
    load_rows(x_ref, held)

    def conv_of(conv, known, part):
        def run(first, count):
            begin = drop * (PITCH + 1) + first * PITCH
            total = convolve(
                patches, w_ref.at[conv], EARLY, known[begin : begin + count * PITCH, :],
                first, count,
            )
            return split_off(part)(total, first, count)

        return run

    body(
        halo, height, width, g_ref, held, flat, patches, nothing,
        conv_of(0, known_one, one_ref), conv_of(1, known_two, two_ref), o_ref, CHUNK,
    )
    keep_tile(o_ref, r_ref)


def late_kernel(
    halo, height, width, x_ref, one_ref, two_ref, w_ref, g_ref, p_ref,
    o_ref, r_ref, held, flat, patches,
):
    load_rows(x_ref, held)
    body(
        halo, height, width, g_ref, held, flat, patches, nothing,
        late_of(patches, w_ref, 0, one_ref), late_of(patches, w_ref, 1, two_ref), o_ref, 4,
    )
    keep_tile(o_ref, r_ref)


def last_kernel(
    halo, height, width, x_ref, one_ref, two_ref, w_ref, g_ref, p_ref, q_ref,
    r_ref, o_ref, held, flat, patches,
):
    late_kernel(
        halo, height, width, x_ref, one_ref, two_ref, w_ref, g_ref, p_ref,
        o_ref, r_ref.at[1], held, flat, patches,
    )


def own_or_passed(kernel, step, former, current, *refs):
    only_at(kernel, step)(*refs)
    pass_on(step, refs[former], refs[current])


def last_or_passed(kernel, step, former, current, *refs):
    refs[current][0] = refs[former + 1][...]
    only_at(kernel, step)(*refs)
    pass_on(step, refs[former], refs[current].at[1])


def pack_kernel(frames, cached, mid, low, high, sems):
    reach = low.shape[1]
    tile = frames.shape[1]
    upper, lower, every = pl.ds(0, reach), pl.ds(tile - reach, reach), pl.ds(0, tile)
    copies = []
    for out, rows in (
        (low, lower), (high, upper), (mid, every),
    ):
        for part, offset in ((frames, 0), (cached, 2)):
            copies.append(
                pltpu.make_async_copy(
                    part.at[:, rows],
                    out.at[pl.ds(offset, part.shape[0])],
                    sems.at[len(copies)],
                )
            )
    for copy in copies:
        copy.start()
    for copy in copies:
        copy.wait()


def sides_kernel(mid, low, high, left, right):
    reach = low.shape[1]
    tile = mid.shape[1]
    for out, begin in ((left, tile - reach), (right, 0)):
        cut = slice(begin, begin + reach)
        out[:, :reach] = low[:, :, cut, :]
        out[:, reach : reach + tile] = mid[:, :, cut, :]
        out[:, reach + tile :] = high[:, :, cut, :]


WHOLE = pl.BlockSpec(memory_space=pltpu.VMEM)


def shaped(*shape, dtype=jnp.bfloat16):
    return jax.ShapeDtypeStruct(shape, dtype)


def launch(kernel, arguments, outs, scratch, span, frames):
    channels = arguments[0].shape[-1]
    return pl.pallas_call(
        kernel,
        out_shape=outs,
        in_specs=[WHOLE] * len(arguments),
        out_specs=[WHOLE] * len(outs),
        scratch_shapes=scratch,
        cost_estimate=pl.CostEstimate(
            flops=4 * 9 * frames * span * PITCH * channels * 2 * channels,
            bytes_accessed=2 << 20,
            transcendentals=0,
        ),
        compiler_params=pltpu.CompilerParams(vmem_limit_bytes=40 << 20),
    )(*arguments)


def room(span):
    return (span + 3) * PITCH


def scratches(span, frames, blocks, channels):
    grid = (room(span), channels)
    return [
        pltpu.VMEM(grid if frames == 1 else (frames,) + grid, jnp.float32),
        pltpu.VMEM(grid, jnp.float32),
        pltpu.VMEM((room(span), blocks * 3 * channels), jnp.bfloat16),
    ]


def parts_of(span, lanes):
    return [
        shaped((span - 2) * PITCH, lanes, dtype=jnp.float32),
        shaped((span - 4) * PITCH, lanes, dtype=jnp.float32),
    ]


def packed(frames, cached, halo):
    tile = (6,) + frames.shape[1:]
    shape = (6, halo) + frames.shape[2:]
    return pl.pallas_call(
        pack_kernel,
        out_shape=[shaped(*tile), shaped(*shape), shaped(*shape)],
        in_specs=[pl.BlockSpec(memory_space=pltpu.HBM)] * 2,
        out_specs=[WHOLE] * 3,
        scratch_shapes=[pltpu.SemaphoreType.DMA((6,))],
        compiler_params=pltpu.CompilerParams(vmem_limit_bytes=PACK_ROOM),
    )(*(pltpu.with_memory_space_constraint(part, pltpu.HBM) for part in (frames, cached)))


def cut_sides(mid, low, high):
    halo = low.shape[1]
    tile, channels = mid.shape[1], mid.shape[-1]
    return pl.pallas_call(
        sides_kernel,
        out_shape=[shaped(6, tile + 2 * halo, halo, channels)] * 2,
        in_specs=[WHOLE] * 3,
        out_specs=[WHOLE] * 2,
        compiler_params=pltpu.CompilerParams(vmem_limit_bytes=8 << 20),
    )(mid, low, high)


def moved(value, segments, shift):
    sizes = [lax.axis_size(axis) for axis in AXES]
    pairs = []
    for segment in segments:
        for row in range(sizes[1]):
            for col in range(sizes[2]):
                target = (segment + shift[0], row + shift[1], col + shift[2])
                if all(0 <= t < n for t, n in zip(target, sizes)):
                    source = (segment * sizes[1] + row) * sizes[2] + col
                    place = (target[0] * sizes[1] + target[1]) * sizes[2] + target[2]
                    pairs.append((source, place))
    return lax.ppermute(value, AXES, pairs)


def ends(parts, cut):
    taken = [cut(part) for part in parts]
    return taken[0] if len(taken) == 1 else jnp.concatenate(taken, axis=0)


def rows_of(parts, segments, halo):
    low = moved(
        ends(parts, lambda part: part[:, part.shape[1] - halo :]), segments, (0, 1, 0)
    )
    high = moved(ends(parts, lambda part: part[:, :halo]), segments, (0, -1, 0))
    return low, high


def sides_of(parts, low, high, halo):
    def side(cut):
        return jnp.concatenate([cut(low), ends(parts, cut), cut(high)], axis=1)

    return side(lambda part: part[:, :, part.shape[2] - halo :]), side(
        lambda part: part[:, :, :halo]
    )


def columns_of(left, right, segments):
    return moved(left, segments, (0, 0, 1)), moved(right, segments, (0, 0, -1))


def on_device(height, width, frames, caches, weights, biases, gains):
    sections = lax.axis_size("segment")
    tile, channels = frames.shape[1], frames.shape[-1]
    kernels = weights[0].reshape((2, 3, 3, 3 * channels, channels))
    bias, gain = biases[0], gains[0]
    cached = caches[0].reshape((4,) + frames.shape[1:])
    halo = 2 * sections
    reach = halo - 2
    others = list(range(1, sections))
    mid, low, high = packed(frames, cached, halo)
    low, high = moved(low, [0], (0, 1, 0)), moved(high, [0], (0, -1, 0))
    left, right = cut_sides(mid, low, high)
    left, right = columns_of(left, right, [0])
    left, later = lax.optimization_barrier((left, mid))
    later = later[2:]
    pieces = (mid, low, high, left, right)
    low, high = rows_of([later], others, reach)
    left, right = sides_of([later], low, high, reach)
    ahead = (low, high) + columns_of(left, right, others)

    span = tile + 2 * halo
    owned = shaped(tile, tile, channels)
    onward = shaped(span - 4, span - 4, channels)
    sent, result, one, two = launch(
        only_at(functools.partial(opening_kernel, halo, height, width), 0),
        pieces + (kernels, bias, gain),
        [onward, owned] + parts_of(span, channels),
        scratches(span, 5, 3, channels), span, 3,
    )
    received = moved(sent, [0], (1, 0, 0))
    sent, result_late = launch(
        only_at(functools.partial(opening_late_kernel, halo, height, width), 0),
        pieces + (kernels, gain, one, two),
        [onward, owned],
        scratches(span, 1, 1, channels), span, 1,
    )
    sent, cached = lax.optimization_barrier((sent, cached))
    received_late = moved(sent, [0], (1, 0, 0))
    span = tile + 2 * reach
    known = launch(
        held_kernel,
        (cached,) + ahead + (kernels, bias),
        parts_of(span, 2 * channels),
        [
            pltpu.VMEM((4, room(span), channels), jnp.float32),
            pltpu.VMEM((room(span), 6 * channels), jnp.bfloat16),
        ],
        span, 2,
    )
    halo = reach
    for step in others:
        span = tile + 2 * halo
        onward = shaped(span - 4, span - 4, channels)
        last = step + 1 == sections
        kernel = functools.partial(early_kernel, halo, reach - halo, height, width)
        outs = [owned] + parts_of(span, channels)
        scratch = scratches(span, 1, 1, channels)
        if last:
            scratch = [pltpu.VMEM(onward.shape, jnp.bfloat16)] + scratch
        else:
            outs = outs + [onward]
        result, one, two, *sent = launch(
            functools.partial(own_or_passed, kernel, step, 5, 6),
            (received, *known, kernels, gain, result),
            outs, scratch, span, 1,
        )
        if last:
            (result,) = launch(
                functools.partial(
                    last_or_passed,
                    functools.partial(last_kernel, halo, height, width),
                    step, 5, 7,
                ),
                (received_late, one, two, kernels, gain, result_late, result),
                [shaped(2, tile, tile, channels)],
                [pltpu.VMEM(onward.shape, jnp.bfloat16)] + scratches(span, 1, 1, channels),
                span, 1,
            )
        else:
            received = moved(sent[0], [step], (1, 0, 0))
            sent, result_late = launch(
                functools.partial(
                    own_or_passed,
                    functools.partial(late_kernel, halo, height, width),
                    step, 5, 7,
                ),
                (received_late, one, two, kernels, gain, result_late),
                [onward, owned],
                scratches(span, 1, 1, channels), span, 1,
            )
            received_late = moved(sent, [step], (1, 0, 0))
        halo = halo - 2
    return result[None]


def solution(mesh):
    height = 16 * mesh.shape["row"]
    width = 16 * mesh.shape["col"]
    in_specs = (
        P(None, "row", "col", None),
        P("segment", None, None, "row", "col", None),
        P("segment", None, None, None, None, None, None),
        P("segment", None, None),
        P("segment", None, None),
    )
    out_specs = P("segment", None, "row", "col", None)
    return jax.shard_map(
        functools.partial(on_device, height, width),
        mesh=mesh, in_specs=in_specs, out_specs=out_specs, check_vma=False,
    )
```

```python
import functools

import jax
import jax.numpy as jnp
from jax import lax
from jax.experimental import pallas as pl
from jax.experimental.pallas import tpu as pltpu
from jax.sharding import PartitionSpec as P

PITCH = 32


def pitch_of(span):
    return -(-span // 8) * 8


PACK_ROOM = 4 << 20
CHUNK = 8
AXES = ("segment", "row", "col")


def norm_act(values, half_gain, mask):
    scale = lax.rsqrt(jnp.mean(values * values, axis=-1, keepdims=True) + 1e-06)
    half = values * scale * half_gain
    return (half + half * jnp.tanh(half)) * mask


def chunks(rows, size=CHUNK):
    return [(first, min(size, rows - first)) for first in range(0, rows, size)]


def column_mask(side, width, channels, pitch):
    col = lax.broadcasted_iota(jnp.int32, (pitch, channels), 0) + side
    return jnp.where((col >= 0) & (col < width), 1.0, 0.0)


def cell_mask(columns, top, height, first, count):
    parts = []
    for row in range(first, first + count):
        here = top + row
        parts.append(columns * jnp.where((here >= 0) & (here < height), 1.0, 0.0))
    return jnp.concatenate(parts, axis=0)


def spread(source, start, patches, block, rows, pitch):
    channels = source.shape[-1]
    for tap in range(3):
        lane = (block * 3 + tap) * channels
        begin = start + tap
        patches[: rows * pitch, lane : lane + channels] = source[
            begin : begin + rows * pitch, :
        ].astype(jnp.bfloat16)


def weight_rows(kernel, tap, sides):
    empty = jnp.zeros(kernel.shape[2:], jnp.bfloat16)

    def column(taps):
        parts = [empty if t is None else kernel[t, tap] for t in taps]
        return parts[0] if len(parts) == 1 else jnp.concatenate(parts, axis=0)

    columns = [column(taps) for taps in sides]
    return columns[0] if len(columns) == 1 else jnp.concatenate(columns, axis=1)


HELD = ((0, 1), (None, 0))
OPENING = ((0, 1, 2), (None, 0, 1))
EARLY = ((2,), (1,))
LATE = ((2,),)


def convolve(patches, kernel, sides, total, first, rows, pitch):
    count = rows * pitch
    starts = [(first + tap) * pitch for tap in range(3)]
    cells = jnp.concatenate([patches[begin : begin + count, :] for begin in starts], axis=1)
    weight = jnp.concatenate([weight_rows(kernel, tap, sides) for tap in range(3)], axis=0)
    return total + jnp.dot(cells, weight, preferred_element_type=jnp.float32)


def bias_of(bias, count):
    return jnp.broadcast_to(
        jnp.concatenate([bias, bias], axis=1), (count, 2 * bias.shape[-1])
    )


def assemble(grid, source, mid, low, high, left, right):
    reach = low.shape[1]
    tile = mid.shape[1]
    for row in range(tile + 2 * reach):
        begin = row * PITCH
        if row < reach:
            body = low[source, row]
        elif row < reach + tile:
            body = mid[source, row - reach]
        else:
            body = high[source, row - reach - tile]
        grid[begin : begin + reach, :] = left[source, row].astype(jnp.float32)
        grid[begin + reach : begin + reach + tile, :] = body.astype(jnp.float32)
        grid[begin + reach + tile : begin + 2 * reach + tile, :] = right[
            source, row
        ].astype(jnp.float32)


def normed(margin, height, width, values_of, gain, flat, rows, span, size, pitch):
    channels = gain.shape[-1]
    tile = span - 2 * margin
    top = lax.axis_index("row") * tile - margin
    columns = column_mask(lax.axis_index("col") * tile - margin, width, channels, pitch)
    half_gain = 0.5 * gain
    for first, count in chunks(rows, size):
        keep = cell_mask(columns, top, height, first, count)
        flat[first * pitch : (first + count) * pitch, :] = norm_act(
            values_of(first, count), half_gain, keep
        )


def body(halo, height, width, g_ref, held, flat, patches, fill, hidden_of, branch_of, o_ref, size):
    span = o_ref.shape[0] + 4
    pitch = pitch_of(span)
    blocks = patches.shape[1] // (3 * held.shape[-1])

    def area(ref, first, count):
        return ref[first * pitch : (first + count) * pitch, :]

    normed(
        halo, height, width, lambda first, count: area(held, first, count),
        g_ref[0:1, :], flat, span, span, size, pitch,
    )
    fill(0)
    spread(flat, 0, patches, blocks - 1, span, pitch)
    normed(
        halo - 1, height, width, hidden_of, g_ref[1:2, :], flat, span - 2, span - 2, size, pitch,
    )
    fill(1)
    spread(flat, 0, patches, blocks - 1, span - 2, pitch)
    for first, count in chunks(span - 4, size):
        offset = (first + 2) * pitch + 2
        out = held[offset : offset + count * pitch, :] + branch_of(first, count)
        for row in range(count):
            o_ref[first + row] = out[row * pitch : row * pitch + span - 4].astype(
                jnp.bfloat16
            )


def split_off(part, pitch):
    def apply(total, first, count):
        channels = part.shape[-1]
        part[first * pitch : (first + count) * pitch, :] = total[:, channels:]
        return total[:, :channels]

    return apply


def only_at(kernel, step):
    def run(*refs):
        @pl.when(lax.axis_index("segment") == step)
        def _():
            kernel(*refs)

    return run


def keep_tile(o_ref, r_ref):
    tile = r_ref.shape[0]
    edge = (o_ref.shape[0] - tile) // 2
    r_ref[...] = o_ref[edge : edge + tile, edge : edge + tile, :]


def pass_on(step, p_ref, r_ref):
    @pl.when(lax.axis_index("segment") != step)
    def _():
        r_ref[...] = p_ref[...]


def opening_kernel(
    halo, height, width, mid, low, high, left, right, w_ref, b_ref, g_ref,
    o_ref, r_ref, one_ref, two_ref, grid, flat, patches,
):
    for slot, source in enumerate((0, 2, 3, 4, 5)):
        assemble(grid.at[slot], source, mid, low, high, left, right)
    span = mid.shape[1] + 2 * halo

    def fill(conv):
        for frame in range(2):
            spread(
                grid.at[1 + 2 * conv + frame], conv * (PITCH + 1), patches, frame,
                span - 2 * conv, PITCH,
            )

    def conv_of(conv, part):
        def run(first, count):
            bias = bias_of(b_ref[conv : conv + 1, :], count * PITCH)
            total = convolve(patches, w_ref.at[conv], OPENING, bias, first, count, PITCH)
            return split_off(part, PITCH)(total, first, count)

        return run

    body(
        halo, height, width, g_ref, grid.at[0], flat, patches, fill,
        conv_of(0, one_ref), conv_of(1, two_ref), o_ref, 10,
    )
    keep_tile(o_ref, r_ref)


def nothing(conv):
    del conv


def late_of(patches, w_ref, conv, part, span):
    pitch = pitch_of(span)

    def run(first, count):
        known = part[first * pitch : (first + count) * pitch, :]
        return convolve(patches, w_ref.at[conv], LATE, known, first, count, pitch)

    return run


def opening_late_kernel(
    halo, height, width, mid, low, high, left, right, w_ref, g_ref,
    one_ref, two_ref, o_ref, r_ref, held, flat, patches,
):
    assemble(held, 1, mid, low, high, left, right)
    body(
        halo, height, width, g_ref, held, flat, patches, nothing,
        late_of(patches, w_ref, 0, one_ref, o_ref.shape[0] + 4),
        late_of(patches, w_ref, 1, two_ref, o_ref.shape[0] + 4), o_ref, 4,
    )
    keep_tile(o_ref, r_ref)


def held_kernel(
    cached, low, high, left, right, w_ref, b_ref, one_ref, two_ref, grid, patches
):
    @pl.when(lax.axis_index("segment") != 0)
    def _():
        add_held(
            cached, low, high, left, right, w_ref, b_ref, one_ref, two_ref, grid, patches
        )


def add_held(
    cached, low, high, left, right, w_ref, b_ref, one_ref, two_ref, grid, patches
):
    span = cached.shape[1] + 2 * low.shape[1]
    for frame in range(4):
        assemble(grid.at[frame], frame, cached, low, high, left, right)
    for conv, out in ((0, one_ref), (1, two_ref)):
        start = conv * (PITCH + 1)
        rows = span - 2 * conv
        for frame in range(2):
            spread(grid.at[2 * conv + frame], start, patches, frame, rows, PITCH)
        for first, count in chunks(rows - 2):
            out[first * PITCH : (first + count) * PITCH, :] = convolve(
                patches, w_ref.at[conv], HELD,
                bias_of(b_ref[conv : conv + 1, :], count * PITCH), first, count, PITCH,
            )


def load_rows(x_ref, held):
    span = x_ref.shape[0]
    pitch = pitch_of(span)
    for row in range(span):
        held[row * pitch : row * pitch + span, :] = x_ref[row].astype(jnp.float32)


def early_kernel(
    halo, drop, height, width, x_ref, known_one, known_two, w_ref, g_ref, p_ref,
    r_ref, one_ref, two_ref, o_ref, held, flat, patches,
):
    load_rows(x_ref, held)
    pitch = pitch_of(x_ref.shape[0])

    def conv_of(conv, known, part):
        def run(first, count):
            begins = [(drop + row) * PITCH + drop for row in range(first, first + count)]
            total = jnp.concatenate(
                [known[begin : begin + pitch, :] for begin in begins], axis=0
            )
            total = convolve(patches, w_ref.at[conv], EARLY, total, first, count, pitch)
            return split_off(part, pitch)(total, first, count)

        return run

    body(
        halo, height, width, g_ref, held, flat, patches, nothing,
        conv_of(0, known_one, one_ref), conv_of(1, known_two, two_ref), o_ref, CHUNK,
    )
    keep_tile(o_ref, r_ref)


def late_kernel(
    halo, height, width, x_ref, one_ref, two_ref, w_ref, g_ref, p_ref,
    o_ref, r_ref, held, flat, patches,
):
    load_rows(x_ref, held)
    body(
        halo, height, width, g_ref, held, flat, patches, nothing,
        late_of(patches, w_ref, 0, one_ref, o_ref.shape[0] + 4),
        late_of(patches, w_ref, 1, two_ref, o_ref.shape[0] + 4), o_ref, 4,
    )
    keep_tile(o_ref, r_ref)


def last_kernel(
    halo, height, width, x_ref, one_ref, two_ref, w_ref, g_ref, p_ref, q_ref,
    r_ref, o_ref, held, flat, patches,
):
    late_kernel(
        halo, height, width, x_ref, one_ref, two_ref, w_ref, g_ref, p_ref,
        o_ref, r_ref.at[1], held, flat, patches,
    )


def own_or_passed(kernel, step, former, current, *refs):
    only_at(kernel, step)(*refs)
    pass_on(step, refs[former], refs[current])


def last_or_passed(kernel, step, former, current, *refs):
    refs[current][0] = refs[former + 1][...]
    only_at(kernel, step)(*refs)
    pass_on(step, refs[former], refs[current].at[1])


def pack_kernel(frames, cached, mid, low, high, sems):
    reach = low.shape[1]
    tile = frames.shape[1]
    upper, lower, every = pl.ds(0, reach), pl.ds(tile - reach, reach), pl.ds(0, tile)
    copies = []
    for out, rows in (
        (low, lower), (high, upper), (mid, every),
    ):
        for part, offset in ((frames, 0), (cached, 2)):
            copies.append(
                pltpu.make_async_copy(
                    part.at[:, rows],
                    out.at[pl.ds(offset, part.shape[0])],
                    sems.at[len(copies)],
                )
            )
    for copy in copies:
        copy.start()
    for copy in copies:
        copy.wait()


def sides_kernel(mid, low, high, left, right):
    reach = low.shape[1]
    tile = mid.shape[1]
    for out, begin in ((left, tile - reach), (right, 0)):
        cut = slice(begin, begin + reach)
        out[:, :reach] = low[:, :, cut, :]
        out[:, reach : reach + tile] = mid[:, :, cut, :]
        out[:, reach + tile :] = high[:, :, cut, :]


WHOLE = pl.BlockSpec(memory_space=pltpu.VMEM)


def shaped(*shape, dtype=jnp.bfloat16):
    return jax.ShapeDtypeStruct(shape, dtype)


def launch(kernel, arguments, outs, scratch, span, frames):
    channels = arguments[0].shape[-1]
    return pl.pallas_call(
        kernel,
        out_shape=outs,
        in_specs=[WHOLE] * len(arguments),
        out_specs=[WHOLE] * len(outs),
        scratch_shapes=scratch,
        cost_estimate=pl.CostEstimate(
            flops=4 * 9 * frames * span * PITCH * channels * 2 * channels,
            bytes_accessed=2 << 20,
            transcendentals=0,
        ),
        compiler_params=pltpu.CompilerParams(vmem_limit_bytes=40 << 20),
    )(*arguments)


def room(span):
    return (span + 3) * PITCH


def scratches(span, frames, blocks, channels):
    grid = (room(span), channels)
    return [
        pltpu.VMEM(grid if frames == 1 else (frames,) + grid, jnp.float32),
        pltpu.VMEM(grid, jnp.float32),
        pltpu.VMEM((room(span), blocks * 3 * channels), jnp.bfloat16),
    ]


def parts_of(span, lanes):
    return [
        shaped((span - 2) * pitch_of(span), lanes, dtype=jnp.float32),
        shaped((span - 4) * pitch_of(span), lanes, dtype=jnp.float32),
    ]


def packed(frames, cached, halo):
    tile = (6,) + frames.shape[1:]
    shape = (6, halo) + frames.shape[2:]
    return pl.pallas_call(
        pack_kernel,
        out_shape=[shaped(*tile), shaped(*shape), shaped(*shape)],
        in_specs=[pl.BlockSpec(memory_space=pltpu.HBM)] * 2,
        out_specs=[WHOLE] * 3,
        scratch_shapes=[pltpu.SemaphoreType.DMA((6,))],
        compiler_params=pltpu.CompilerParams(vmem_limit_bytes=PACK_ROOM),
    )(*(pltpu.with_memory_space_constraint(part, pltpu.HBM) for part in (frames, cached)))


def cut_sides(mid, low, high):
    halo = low.shape[1]
    tile, channels = mid.shape[1], mid.shape[-1]
    return pl.pallas_call(
        sides_kernel,
        out_shape=[shaped(6, tile + 2 * halo, halo, channels)] * 2,
        in_specs=[WHOLE] * 3,
        out_specs=[WHOLE] * 2,
        compiler_params=pltpu.CompilerParams(vmem_limit_bytes=8 << 20),
    )(mid, low, high)


def moved(value, segments, shift):
    sizes = [lax.axis_size(axis) for axis in AXES]
    pairs = []
    for segment in segments:
        for row in range(sizes[1]):
            for col in range(sizes[2]):
                target = (segment + shift[0], row + shift[1], col + shift[2])
                if all(0 <= t < n for t, n in zip(target, sizes)):
                    source = (segment * sizes[1] + row) * sizes[2] + col
                    place = (target[0] * sizes[1] + target[1]) * sizes[2] + target[2]
                    pairs.append((source, place))
    return lax.ppermute(value, AXES, pairs)


def ends(parts, cut):
    taken = [cut(part) for part in parts]
    return taken[0] if len(taken) == 1 else jnp.concatenate(taken, axis=0)


def rows_of(parts, segments, halo):
    low = moved(
        ends(parts, lambda part: part[:, part.shape[1] - halo :]), segments, (0, 1, 0)
    )
    high = moved(ends(parts, lambda part: part[:, :halo]), segments, (0, -1, 0))
    return low, high


def sides_of(parts, low, high, halo):
    def side(cut):
        return jnp.concatenate([cut(low), ends(parts, cut), cut(high)], axis=1)

    return side(lambda part: part[:, :, part.shape[2] - halo :]), side(
        lambda part: part[:, :, :halo]
    )


def columns_of(left, right, segments):
    return moved(left, segments, (0, 0, 1)), moved(right, segments, (0, 0, -1))


def on_device(height, width, frames, caches, weights, biases, gains):
    sections = lax.axis_size("segment")
    tile, channels = frames.shape[1], frames.shape[-1]
    kernels = weights[0].reshape((2, 3, 3, 3 * channels, channels))
    bias, gain = biases[0], gains[0]
    cached = caches[0].reshape((4,) + frames.shape[1:])
    halo = 2 * sections
    reach = halo - 2
    others = list(range(1, sections))
    mid, low, high = packed(frames, cached, halo)
    low, high = moved(low, [0], (0, 1, 0)), moved(high, [0], (0, -1, 0))
    left, right = cut_sides(mid, low, high)
    left, right = columns_of(left, right, [0])
    left, later = lax.optimization_barrier((left, mid))
    later = later[2:]
    pieces = (mid, low, high, left, right)
    low, high = rows_of([later], others, reach)
    left, right = sides_of([later], low, high, reach)
    ahead = (low, high) + columns_of(left, right, others)

    span = tile + 2 * halo
    owned = shaped(tile, tile, channels)
    onward = shaped(span - 4, span - 4, channels)
    sent, result, one, two = launch(
        only_at(functools.partial(opening_kernel, halo, height, width), 0),
        pieces + (kernels, bias, gain),
        [onward, owned] + parts_of(span, channels),
        scratches(span, 5, 3, channels), span, 3,
    )
    received = moved(sent, [0], (1, 0, 0))
    sent, result_late = launch(
        only_at(functools.partial(opening_late_kernel, halo, height, width), 0),
        pieces + (kernels, gain, one, two),
        [onward, owned],
        scratches(span, 1, 1, channels), span, 1,
    )
    sent, cached = lax.optimization_barrier((sent, cached))
    received_late = moved(sent, [0], (1, 0, 0))
    span = tile + 2 * reach
    known = launch(
        held_kernel,
        (cached,) + ahead + (kernels, bias),
        parts_of(span, 2 * channels),
        [
            pltpu.VMEM((4, room(span), channels), jnp.float32),
            pltpu.VMEM((room(span), 6 * channels), jnp.bfloat16),
        ],
        span, 2,
    )
    halo = reach
    for step in others:
        span = tile + 2 * halo
        onward = shaped(span - 4, span - 4, channels)
        last = step + 1 == sections
        kernel = functools.partial(early_kernel, halo, reach - halo, height, width)
        outs = [owned] + parts_of(span, channels)
        scratch = scratches(span, 1, 1, channels)
        if last:
            scratch = [pltpu.VMEM(onward.shape, jnp.bfloat16)] + scratch
        else:
            outs = outs + [onward]
        result, one, two, *sent = launch(
            functools.partial(own_or_passed, kernel, step, 5, 6),
            (received, *known, kernels, gain, result),
            outs, scratch, span, 1,
        )
        if last:
            (result,) = launch(
                functools.partial(
                    last_or_passed,
                    functools.partial(last_kernel, halo, height, width),
                    step, 5, 7,
                ),
                (received_late, one, two, kernels, gain, result_late, result),
                [shaped(2, tile, tile, channels)],
                [pltpu.VMEM(onward.shape, jnp.bfloat16)] + scratches(span, 1, 1, channels),
                span, 1,
            )
        else:
            received = moved(sent[0], [step], (1, 0, 0))
            sent, result_late = launch(
                functools.partial(
                    own_or_passed,
                    functools.partial(late_kernel, halo, height, width),
                    step, 5, 7,
                ),
                (received_late, one, two, kernels, gain, result_late),
                [onward, owned],
                scratches(span, 1, 1, channels), span, 1,
            )
            received_late = moved(sent, [step], (1, 0, 0))
        halo = halo - 2
    return result[None]


def solution(mesh):
    height = 16 * mesh.shape["row"]
    width = 16 * mesh.shape["col"]
    in_specs = (
        P(None, "row", "col", None),
        P("segment", None, None, "row", "col", None),
        P("segment", None, None, None, None, None, None),
        P("segment", None, None),
        P("segment", None, None),
    )
    out_specs = P("segment", None, "row", "col", None)
    return jax.shard_map(
        functools.partial(on_device, height, width),
        mesh=mesh, in_specs=in_specs, out_specs=out_specs, check_vma=False,
    )
```

```python
import functools

import jax
import jax.numpy as jnp
from jax import lax
from jax.experimental import pallas as pl
from jax.experimental.pallas import tpu as pltpu
from jax.sharding import PartitionSpec as P

PITCH = 32


def pitch_of(span):
    return -(-span // 8) * 8


PACK_ROOM = 4 << 20
CHUNK = 8
AXES = ("segment", "row", "col")


def norm_act(values, half_gain, mask):
    scale = lax.rsqrt(jnp.mean(values * values, axis=-1, keepdims=True) + 1e-06)
    half = values * scale * half_gain
    return (half + half * jnp.tanh(half)) * mask


def chunks(rows, size=CHUNK):
    return [(first, min(size, rows - first)) for first in range(0, rows, size)]


def column_mask(side, width, channels, pitch):
    col = lax.broadcasted_iota(jnp.int32, (pitch, channels), 0) + side
    return jnp.where((col >= 0) & (col < width), 1.0, 0.0)


def cell_mask(columns, top, height, first, count):
    parts = []
    for row in range(first, first + count):
        here = top + row
        parts.append(columns * jnp.where((here >= 0) & (here < height), 1.0, 0.0))
    return jnp.concatenate(parts, axis=0)


def spread(source, start, patches, block, rows, pitch):
    channels = source.shape[-1]
    for tap in range(3):
        lane = (block * 3 + tap) * channels
        begin = start + tap
        patches[: rows * pitch, lane : lane + channels] = source[
            begin : begin + rows * pitch, :
        ].astype(jnp.bfloat16)


def weight_rows(kernel, tap, sides):
    empty = jnp.zeros(kernel.shape[2:], jnp.bfloat16)

    def column(taps):
        parts = [empty if t is None else kernel[t, tap] for t in taps]
        return parts[0] if len(parts) == 1 else jnp.concatenate(parts, axis=0)

    columns = [column(taps) for taps in sides]
    return columns[0] if len(columns) == 1 else jnp.concatenate(columns, axis=1)


HELD = ((0, 1), (None, 0))
OPENING = ((0, 1, 2), (None, 0, 1))
EARLY = ((2,), (1,))
LATE = ((2,),)


def convolve(patches, kernel, sides, total, first, rows, pitch):
    count = rows * pitch
    starts = [(first + tap) * pitch for tap in range(3)]
    cells = jnp.concatenate([patches[begin : begin + count, :] for begin in starts], axis=1)
    weight = jnp.concatenate([weight_rows(kernel, tap, sides) for tap in range(3)], axis=0)
    return total + jnp.dot(cells, weight, preferred_element_type=jnp.float32)


def bias_of(bias, count):
    return jnp.broadcast_to(
        jnp.concatenate([bias, bias], axis=1), (count, 2 * bias.shape[-1])
    )


def assemble(grid, source, mid, low, high, left, right):
    reach = low.shape[1]
    tile = mid.shape[1]
    for row in range(tile + 2 * reach):
        begin = row * PITCH
        if row < reach:
            body = low[source, row]
        elif row < reach + tile:
            body = mid[source, row - reach]
        else:
            body = high[source, row - reach - tile]
        grid[begin : begin + reach, :] = left[source, row].astype(jnp.float32)
        grid[begin + reach : begin + reach + tile, :] = body.astype(jnp.float32)
        grid[begin + reach + tile : begin + 2 * reach + tile, :] = right[
            source, row
        ].astype(jnp.float32)


def normed(margin, height, width, values_of, gain, flat, rows, span, size, pitch):
    channels = gain.shape[-1]
    tile = span - 2 * margin
    top = lax.axis_index("row") * tile - margin
    columns = column_mask(lax.axis_index("col") * tile - margin, width, channels, pitch)
    half_gain = 0.5 * gain
    for first, count in chunks(rows, size):
        keep = cell_mask(columns, top, height, first, count)
        flat[first * pitch : (first + count) * pitch, :] = norm_act(
            values_of(first, count), half_gain, keep
        )


def body(halo, height, width, g_ref, held, flat, patches, fill, hidden_of, branch_of, o_ref, size):
    span = o_ref.shape[0] + 4
    pitch = pitch_of(span)
    blocks = patches.shape[1] // (3 * held.shape[-1])

    def area(ref, first, count):
        return ref[first * pitch : (first + count) * pitch, :]

    normed(
        halo, height, width, lambda first, count: area(held, first, count),
        g_ref[0:1, :], flat, span, span, size, pitch,
    )
    fill(0)
    spread(flat, 0, patches, blocks - 1, span, pitch)
    normed(
        halo - 1, height, width, hidden_of, g_ref[1:2, :], flat, span - 2, span - 2, size, pitch,
    )
    fill(1)
    spread(flat, 0, patches, blocks - 1, span - 2, pitch)
    for first, count in chunks(span - 4, size):
        offset = (first + 2) * pitch + 2
        out = held[offset : offset + count * pitch, :] + branch_of(first, count)
        for row in range(count):
            o_ref[first + row] = out[row * pitch : row * pitch + span - 4].astype(
                jnp.bfloat16
            )


def split_off(part, pitch):
    def apply(total, first, count):
        channels = part.shape[-1]
        part[first * pitch : (first + count) * pitch, :] = total[:, channels:]
        return total[:, :channels]

    return apply


def only_at(kernel, step):
    def run(*refs):
        @pl.when(lax.axis_index("segment") == step)
        def _():
            kernel(*refs)

    return run


def keep_tile(o_ref, r_ref):
    tile = r_ref.shape[0]
    edge = (o_ref.shape[0] - tile) // 2
    r_ref[...] = o_ref[edge : edge + tile, edge : edge + tile, :]


def pass_on(step, p_ref, r_ref):
    @pl.when(lax.axis_index("segment") != step)
    def _():
        r_ref[...] = p_ref[...]


def opening_kernel(
    halo, height, width, mid, low, high, left, right, w_ref, b_ref, g_ref,
    o_ref, r_ref, one_ref, two_ref, grid, flat, patches,
):
    for slot, source in enumerate((0, 2, 3, 4, 5)):
        assemble(grid.at[slot], source, mid, low, high, left, right)
    span = mid.shape[1] + 2 * halo

    def fill(conv):
        for frame in range(2):
            spread(
                grid.at[1 + 2 * conv + frame], conv * (PITCH + 1), patches, frame,
                span - 2 * conv, PITCH,
            )

    def conv_of(conv, part):
        def run(first, count):
            bias = bias_of(b_ref[conv : conv + 1, :], count * PITCH)
            total = convolve(patches, w_ref.at[conv], OPENING, bias, first, count, PITCH)
            return split_off(part, PITCH)(total, first, count)

        return run

    body(
        halo, height, width, g_ref, grid.at[0], flat, patches, fill,
        conv_of(0, one_ref), conv_of(1, two_ref), o_ref, 15,
    )
    keep_tile(o_ref, r_ref)


def nothing(conv):
    del conv


def late_of(patches, w_ref, conv, part, span):
    pitch = pitch_of(span)

    def run(first, count):
        known = part[first * pitch : (first + count) * pitch, :]
        return convolve(patches, w_ref.at[conv], LATE, known, first, count, pitch)

    return run


def opening_late_kernel(
    halo, height, width, mid, low, high, left, right, w_ref, g_ref,
    one_ref, two_ref, o_ref, r_ref, held, flat, patches,
):
    assemble(held, 1, mid, low, high, left, right)
    body(
        halo, height, width, g_ref, held, flat, patches, nothing,
        late_of(patches, w_ref, 0, one_ref, o_ref.shape[0] + 4),
        late_of(patches, w_ref, 1, two_ref, o_ref.shape[0] + 4), o_ref, 4,
    )
    keep_tile(o_ref, r_ref)


def held_kernel(
    cached, low, high, left, right, w_ref, b_ref, one_ref, two_ref, grid, patches
):
    @pl.when(lax.axis_index("segment") != 0)
    def _():
        add_held(
            cached, low, high, left, right, w_ref, b_ref, one_ref, two_ref, grid, patches
        )


def add_held(
    cached, low, high, left, right, w_ref, b_ref, one_ref, two_ref, grid, patches
):
    span = cached.shape[1] + 2 * low.shape[1]
    for frame in range(4):
        assemble(grid.at[frame], frame, cached, low, high, left, right)
    for conv, out in ((0, one_ref), (1, two_ref)):
        start = conv * (PITCH + 1)
        rows = span - 2 * conv
        for frame in range(2):
            spread(grid.at[2 * conv + frame], start, patches, frame, rows, PITCH)
        for first, count in chunks(rows - 2):
            out[first * PITCH : (first + count) * PITCH, :] = convolve(
                patches, w_ref.at[conv], HELD,
                bias_of(b_ref[conv : conv + 1, :], count * PITCH), first, count, PITCH,
            )


def load_rows(x_ref, held):
    span = x_ref.shape[0]
    pitch = pitch_of(span)
    for row in range(span):
        held[row * pitch : row * pitch + span, :] = x_ref[row].astype(jnp.float32)


def early_kernel(
    halo, drop, height, width, x_ref, known_one, known_two, w_ref, g_ref, p_ref,
    r_ref, one_ref, two_ref, o_ref, held, flat, patches,
):
    load_rows(x_ref, held)
    pitch = pitch_of(x_ref.shape[0])

    def conv_of(conv, known, part):
        def run(first, count):
            begins = [(drop + row) * PITCH + drop for row in range(first, first + count)]
            total = jnp.concatenate(
                [known[begin : begin + pitch, :] for begin in begins], axis=0
            )
            total = convolve(patches, w_ref.at[conv], EARLY, total, first, count, pitch)
            return split_off(part, pitch)(total, first, count)

        return run

    body(
        halo, height, width, g_ref, held, flat, patches, nothing,
        conv_of(0, known_one, one_ref), conv_of(1, known_two, two_ref), o_ref, CHUNK,
    )
    keep_tile(o_ref, r_ref)


def late_kernel(
    halo, height, width, x_ref, one_ref, two_ref, w_ref, g_ref, p_ref,
    o_ref, r_ref, held, flat, patches,
):
    load_rows(x_ref, held)
    body(
        halo, height, width, g_ref, held, flat, patches, nothing,
        late_of(patches, w_ref, 0, one_ref, o_ref.shape[0] + 4),
        late_of(patches, w_ref, 1, two_ref, o_ref.shape[0] + 4), o_ref, 4,
    )
    keep_tile(o_ref, r_ref)


def last_kernel(
    halo, height, width, x_ref, one_ref, two_ref, w_ref, g_ref, p_ref, q_ref,
    r_ref, o_ref, held, flat, patches,
):
    late_kernel(
        halo, height, width, x_ref, one_ref, two_ref, w_ref, g_ref, p_ref,
        o_ref, r_ref.at[1], held, flat, patches,
    )


def own_or_passed(kernel, step, former, current, *refs):
    only_at(kernel, step)(*refs)
    pass_on(step, refs[former], refs[current])


def last_or_passed(kernel, step, former, current, *refs):
    refs[current][0] = refs[former + 1][...]
    only_at(kernel, step)(*refs)
    pass_on(step, refs[former], refs[current].at[1])


def pack_kernel(frames, cached, mid, low, high, sems):
    reach = low.shape[1]
    tile = frames.shape[1]
    upper, lower, every = pl.ds(0, reach), pl.ds(tile - reach, reach), pl.ds(0, tile)
    copies = []
    for out, rows in (
        (low, lower), (high, upper), (mid, every),
    ):
        for part, offset in ((frames, 0), (cached, 2)):
            copies.append(
                pltpu.make_async_copy(
                    part.at[:, rows],
                    out.at[pl.ds(offset, part.shape[0])],
                    sems.at[len(copies)],
                )
            )
    for copy in copies:
        copy.start()
    for copy in copies:
        copy.wait()


def sides_kernel(mid, low, high, left, right):
    reach = low.shape[1]
    tile = mid.shape[1]
    for out, begin in ((left, tile - reach), (right, 0)):
        cut = slice(begin, begin + reach)
        out[:, :reach] = low[:, :, cut, :]
        out[:, reach : reach + tile] = mid[:, :, cut, :]
        out[:, reach + tile :] = high[:, :, cut, :]


WHOLE = pl.BlockSpec(memory_space=pltpu.VMEM)


def shaped(*shape, dtype=jnp.bfloat16):
    return jax.ShapeDtypeStruct(shape, dtype)


def launch(kernel, arguments, outs, scratch, span, frames):
    channels = arguments[0].shape[-1]
    return pl.pallas_call(
        kernel,
        out_shape=outs,
        in_specs=[WHOLE] * len(arguments),
        out_specs=[WHOLE] * len(outs),
        scratch_shapes=scratch,
        cost_estimate=pl.CostEstimate(
            flops=4 * 9 * frames * span * PITCH * channels * 2 * channels,
            bytes_accessed=2 << 20,
            transcendentals=0,
        ),
        compiler_params=pltpu.CompilerParams(vmem_limit_bytes=40 << 20),
    )(*arguments)


def room(span):
    return (span + 3) * PITCH


def scratches(span, frames, blocks, channels):
    grid = (room(span), channels)
    return [
        pltpu.VMEM(grid if frames == 1 else (frames,) + grid, jnp.float32),
        pltpu.VMEM(grid, jnp.float32),
        pltpu.VMEM((room(span), blocks * 3 * channels), jnp.bfloat16),
    ]


def parts_of(span, lanes):
    return [
        shaped((span - 2) * pitch_of(span), lanes, dtype=jnp.float32),
        shaped((span - 4) * pitch_of(span), lanes, dtype=jnp.float32),
    ]


def packed(frames, cached, halo):
    tile = (6,) + frames.shape[1:]
    shape = (6, halo) + frames.shape[2:]
    return pl.pallas_call(
        pack_kernel,
        out_shape=[shaped(*tile), shaped(*shape), shaped(*shape)],
        in_specs=[pl.BlockSpec(memory_space=pltpu.HBM)] * 2,
        out_specs=[WHOLE] * 3,
        scratch_shapes=[pltpu.SemaphoreType.DMA((6,))],
        compiler_params=pltpu.CompilerParams(vmem_limit_bytes=PACK_ROOM),
    )(*(pltpu.with_memory_space_constraint(part, pltpu.HBM) for part in (frames, cached)))


def cut_sides(mid, low, high):
    halo = low.shape[1]
    tile, channels = mid.shape[1], mid.shape[-1]
    return pl.pallas_call(
        sides_kernel,
        out_shape=[shaped(6, tile + 2 * halo, halo, channels)] * 2,
        in_specs=[WHOLE] * 3,
        out_specs=[WHOLE] * 2,
        compiler_params=pltpu.CompilerParams(vmem_limit_bytes=8 << 20),
    )(mid, low, high)


def moved(value, segments, shift):
    sizes = [lax.axis_size(axis) for axis in AXES]
    pairs = []
    for segment in segments:
        for row in range(sizes[1]):
            for col in range(sizes[2]):
                target = (segment + shift[0], row + shift[1], col + shift[2])
                if all(0 <= t < n for t, n in zip(target, sizes)):
                    source = (segment * sizes[1] + row) * sizes[2] + col
                    place = (target[0] * sizes[1] + target[1]) * sizes[2] + target[2]
                    pairs.append((source, place))
    return lax.ppermute(value, AXES, pairs)


def ends(parts, cut):
    taken = [cut(part) for part in parts]
    return taken[0] if len(taken) == 1 else jnp.concatenate(taken, axis=0)


def rows_of(parts, segments, halo):
    low = moved(
        ends(parts, lambda part: part[:, part.shape[1] - halo :]), segments, (0, 1, 0)
    )
    high = moved(ends(parts, lambda part: part[:, :halo]), segments, (0, -1, 0))
    return low, high


def sides_of(parts, low, high, halo):
    def side(cut):
        return jnp.concatenate([cut(low), ends(parts, cut), cut(high)], axis=1)

    return side(lambda part: part[:, :, part.shape[2] - halo :]), side(
        lambda part: part[:, :, :halo]
    )


def columns_of(left, right, segments):
    return moved(left, segments, (0, 0, 1)), moved(right, segments, (0, 0, -1))


def on_device(height, width, frames, caches, weights, biases, gains):
    sections = lax.axis_size("segment")
    tile, channels = frames.shape[1], frames.shape[-1]
    kernels = weights[0].reshape((2, 3, 3, 3 * channels, channels))
    bias, gain = biases[0], gains[0]
    cached = caches[0].reshape((4,) + frames.shape[1:])
    halo = 2 * sections
    reach = halo - 2
    others = list(range(1, sections))
    mid, low, high = packed(frames, cached, halo)
    low, high = moved(low, [0], (0, 1, 0)), moved(high, [0], (0, -1, 0))
    left, right = cut_sides(mid, low, high)
    left, right = columns_of(left, right, [0])
    left, later = lax.optimization_barrier((left, mid))
    later = later[2:]
    pieces = (mid, low, high, left, right)
    low, high = rows_of([later], others, reach)
    left, right = sides_of([later], low, high, reach)
    ahead = (low, high) + columns_of(left, right, others)

    span = tile + 2 * halo
    owned = shaped(tile, tile, channels)
    onward = shaped(span - 4, span - 4, channels)
    sent, result, one, two = launch(
        only_at(functools.partial(opening_kernel, halo, height, width), 0),
        pieces + (kernels, bias, gain),
        [onward, owned] + parts_of(span, channels),
        scratches(span, 5, 3, channels), span, 3,
    )
    received = moved(sent, [0], (1, 0, 0))
    sent, result_late = launch(
        only_at(functools.partial(opening_late_kernel, halo, height, width), 0),
        pieces + (kernels, gain, one, two),
        [onward, owned],
        scratches(span, 1, 1, channels), span, 1,
    )
    sent, cached = lax.optimization_barrier((sent, cached))
    received_late = moved(sent, [0], (1, 0, 0))
    span = tile + 2 * reach
    known = launch(
        held_kernel,
        (cached,) + ahead + (kernels, bias),
        parts_of(span, 2 * channels),
        [
            pltpu.VMEM((4, room(span), channels), jnp.float32),
            pltpu.VMEM((room(span), 6 * channels), jnp.bfloat16),
        ],
        span, 2,
    )
    halo = reach
    for step in others:
        span = tile + 2 * halo
        onward = shaped(span - 4, span - 4, channels)
        last = step + 1 == sections
        kernel = functools.partial(early_kernel, halo, reach - halo, height, width)
        outs = [owned] + parts_of(span, channels)
        scratch = scratches(span, 1, 1, channels)
        if last:
            scratch = [pltpu.VMEM(onward.shape, jnp.bfloat16)] + scratch
        else:
            outs = outs + [onward]
        result, one, two, *sent = launch(
            functools.partial(own_or_passed, kernel, step, 5, 6),
            (received, *known, kernels, gain, result),
            outs, scratch, span, 1,
        )
        if last:
            (result,) = launch(
                functools.partial(
                    last_or_passed,
                    functools.partial(last_kernel, halo, height, width),
                    step, 5, 7,
                ),
                (received_late, one, two, kernels, gain, result_late, result),
                [shaped(2, tile, tile, channels)],
                [pltpu.VMEM(onward.shape, jnp.bfloat16)] + scratches(span, 1, 1, channels),
                span, 1,
            )
        else:
            received = moved(sent[0], [step], (1, 0, 0))
            sent, result_late = launch(
                functools.partial(
                    own_or_passed,
                    functools.partial(late_kernel, halo, height, width),
                    step, 5, 7,
                ),
                (received_late, one, two, kernels, gain, result_late),
                [onward, owned],
                scratches(span, 1, 1, channels), span, 1,
            )
            received_late = moved(sent, [step], (1, 0, 0))
        halo = halo - 2
    return result[None]


def solution(mesh):
    height = 16 * mesh.shape["row"]
    width = 16 * mesh.shape["col"]
    in_specs = (
        P(None, "row", "col", None),
        P("segment", None, None, "row", "col", None),
        P("segment", None, None, None, None, None, None),
        P("segment", None, None),
        P("segment", None, None),
    )
    out_specs = P("segment", None, "row", "col", None)
    return jax.shard_map(
        functools.partial(on_device, height, width),
        mesh=mesh, in_specs=in_specs, out_specs=out_specs, check_vma=False,
    )
```
